128 devices in a mesh: seq: 32 (over x, y, core), head: 4 (over z).
Axes of the slice: x: 4, y: 4, z: 4, core: 2. Of those that a mesh axis runs over, the one named last changes fastest.
Arguments:
- vis_tokens: bfloat16 [12288, 1408], P('seq'), may hold values from -70 to 70
- vis_counts: int32 [4, 8], replicated, may hold values from 1 to 384, 1536 in all within a row
- vis_spatial: int32 [4, 96], replicated, may hold values from 0 to 1023, as said below
- enc_gain: float32 [1408], replicated, may hold values from 0.25 to 1.75
- enc_bias: float32 [1408], replicated, may hold values from -3 to 3
- enc_qkv: bfloat16 [3, 1408, 1408], P(None, None, 'head'), may hold values from -6 to 6
- enc_proj: bfloat16 [1408, 1408], P('head'), may hold values from -0.15625 to 0.15625
- final_gain: float32 [1408], replicated, may hold values from 0.25 to 1.75
- final_bias: float32 [1408], replicated, may hold values from -3 to 3
- to_decoder: bfloat16 [1408, 512], replicated, may hold values from -0.15625 to 0.15625
- mask_token: float32 [512], replicated, may hold values from -4 to 4
- dec_gain: float32 [512], replicated, may hold values from 0.25 to 1.75
- dec_bias: float32 [512], replicated, may hold values from -3 to 3
- dec_qkv: bfloat16 [3, 512, 512], P(None, None, 'head'), may hold values from -11 to 11
Outputs:
- decoded: bfloat16 [4, 16, 1024, 512], P(None, None, 'seq', 'head')
The draws below stay inside these ranges and needn't reach their ends.
Inputs may be any that keep to these rules, and one draw needn't show every extreme that they name: `vis_spatial`: row c lists in increasing order the spatial positions visible in every frame of clip c; each aligned run of 32 spatial positions holds exactly 3 of them. The visible tokens of clip c, in order of position, lie on the members of its encoder group in order, vis_counts[c, g] of them on member g; each row sums to 1536.
All inputs are finite; a program needn't handle non-finite values.
Results may differ from the reference program's by a relative error of at most 0.015.
Values may be sent and summed in bfloat16 or wider, within the bound.
A program may use at most 320 MiB of HBM per device.

```python
import math
import jax
import jax.numpy as jnp
import numpy as np
from jax import lax

D = 1408
HEADS = 16
DD = 512
DHEADS = 8
S = 1024
BLOCK = 32
VB = 3
GROUP = 8
L = 16384
VSP = 96
VIS = 1536
VCAP = 384
ENC_SLOTS = 12288
CLIPS = 4
ROUNDS = 16


def draw_vis_spatial(key, part):
    block_count = S // BLOCK
    scores = jax.random.randint(key, (CLIPS, block_count, BLOCK), 0, 1 << 20) * BLOCK + jnp.arange(BLOCK, dtype=jnp.int32)
    order = jnp.argsort(scores, axis=-1, stable=True)[..., :VB]
    picked = jnp.sort(order, axis=-1) + (jnp.arange(block_count, dtype=jnp.int32) * BLOCK)[None, :, None]
    return picked.reshape(CLIPS, VSP).astype(jnp.int32)


def draw_vis_tokens(key, part):
    first_key = jax.random.fold_in(key, 0)
    base_rows = jnp.clip(jax.random.normal(first_key, (ENC_SLOTS, D), jnp.float32), -6.0, 6.0) * 0.2
    return base_rows.astype(jnp.bfloat16)


def draw_enc_qkv(key, part):
    first_key = jax.random.fold_in(key, 0)
    weights = jnp.clip(jax.random.normal(first_key, (3, D, D), jnp.float32), -6.0, 6.0) * D ** (-0.5)
    weights = weights.at[0].set(weights[0] * 3.0)
    return weights.astype(jnp.bfloat16)


def draw_dec_qkv(key, part):
    first_key = jax.random.fold_in(key, 0)
    weights = jnp.clip(jax.random.normal(first_key, (3, DD, DD), jnp.float32), -6.0, 6.0) * DD ** (-0.5)
    weights = weights.at[0].set(weights[0] * 3.0)
    return weights.astype(jnp.bfloat16)


def shard_levels(own_key, dims, pieces, low, top_value):
    gain, own = 1.0, jax.random.fold_in(own_key, 6)
    for axis_at, parts in pieces:
        heights = jnp.exp(jax.random.uniform(jax.random.fold_in(own, axis_at), (parts,), jnp.float32, low / len(pieces), top_value / len(pieces)))
        gain = gain * jnp.repeat(heights, dims[axis_at] // parts).reshape([-1 if axis == axis_at else 1 for axis in range(len(dims))])
    return gain


def length_profile(amount, total, most, lean):
    loads = [(1 << 20) // math.isqrt(grade ** lean) + 1 for grade in range(2, amount + 1)]
    spare, given = total - most - (amount - 1), [1] * (amount - 1)
    while spare > 0:
        candidates = [i for i in range(amount - 1) if given[i] < most]
        pool, left = sum([loads[i] for i in candidates]), spare
        for i in candidates:
            extra = min(most - given[i], max(1, left * loads[i] // pool), spare)
            given[i] = given[i] + extra
            spare = spare - extra
    return np.array([most] + given)


def uneven(key, amount, total, reach, skew):
    if amount == 2:
        one = jax.random.randint(key, (), max(1, total - reach), min(reach, total - 1) + 1)
        return jnp.stack([one, total - one])
    sizes = jnp.asarray(length_profile(amount, total, reach, skew), jnp.int32)
    pairs = (amount - 1) // 2
    donor, receiver = sizes[1:1 + 2 * pairs:2], sizes[2:2 + 2 * pairs:2]
    room = jnp.minimum(donor - 1, reach - receiver)
    shifted = jax.random.randint(jax.random.fold_in(key, 1), (pairs,), 0, 1 << 20) % (room + 1)
    sizes = sizes.at[1:1 + 2 * pairs:2].set(donor - shifted).at[2:2 + 2 * pairs:2].set(receiver + shifted)
    return sizes[jax.random.permutation(jax.random.fold_in(key, 2), amount)]


def scatter_about(rng, dims, width, reach, shards=(), kind=jnp.bfloat16):
    values = jax.random.normal(rng, dims, jnp.float32) * width
    if len(shards) > 0:
        values = shard_levels(rng, dims, shards, -0.22, 0.18) * values
    return jnp.clip(values, min=-reach, max=reach).astype(kind)


def setup_inputs(seed: int = 0) -> dict:
    keys = jax.random.split(jax.random.key(seed), 15)
    vis_tokens = draw_vis_tokens(jax.random.fold_in(keys[14], 71), 0)
    vis_counts = jax.vmap(lambda own: uneven(own, GROUP, VIS, VCAP, 2))(jax.random.split(keys[1], CLIPS)).reshape((CLIPS, GROUP)).astype(jnp.int32)
    vis_spatial = draw_vis_spatial(jax.random.fold_in(keys[14], 71), 0)
    enc_gain = jnp.clip(1.0 + 0.15 * jax.random.normal(keys[3], (D,), jnp.float32), 0.25, 1.75)
    enc_bias = scatter_about(keys[4], (D,), 0.5, 3.0, (), jnp.float32)
    enc_qkv = draw_enc_qkv(jax.random.fold_in(keys[14], 71), 0)
    enc_proj = scatter_about(keys[6], (D, D), D ** -0.5, 0.15625, ((0, 4),))
    final_gain = jnp.clip(1.0 + 0.15 * jax.random.normal(keys[7], (D,), jnp.float32), 0.25, 1.75)
    final_bias = scatter_about(keys[8], (D,), 0.5, 3.0, (), jnp.float32)
    to_decoder = scatter_about(keys[9], (D, DD), D ** -0.5, 0.15625)
    mask_token = scatter_about(keys[10], (DD,), 1.0, 4.0, (), jnp.float32)
    dec_gain = jnp.clip(1.0 + 0.15 * jax.random.normal(keys[11], (DD,), jnp.float32), 0.25, 1.75)
    dec_bias = scatter_about(keys[12], (DD,), 0.5, 3.0, (), jnp.float32)
    dec_qkv = draw_dec_qkv(jax.random.fold_in(keys[14], 71), 0)
    return {"vis_tokens": vis_tokens, "vis_counts": vis_counts, "vis_spatial": vis_spatial, "enc_gain": enc_gain, "enc_bias": enc_bias, "enc_qkv": enc_qkv, "enc_proj": enc_proj, "final_gain": final_gain, "final_bias": final_bias, "to_decoder": to_decoder, "mask_token": mask_token, "dec_gain": dec_gain, "dec_bias": dec_bias, "dec_qkv": dec_qkv}


def layer_norm(values, gain_row, bias_row):
    centre = lax.optimization_barrier(jnp.mean(values, axis=-1, keepdims=True))
    centred = values - centre
    spread = lax.optimization_barrier(jnp.mean(centred * centred, axis=-1, keepdims=True))
    return centred * lax.rsqrt(spread + 1e-06) * gain_row + bias_row

def sinusoid(positions, table_width):
    column_ids = jnp.arange(table_width, dtype=jnp.int32)
    exponent = (2 * (column_ids // 2)).astype(jnp.float32) / table_width
    frequency = jnp.exp(exponent * -math.log(10000.0))
    angles = positions.astype(jnp.float32)[:, None] * frequency[None, :]
    return jnp.where(column_ids[None, :] % 2 == 0, jnp.sin(angles), jnp.cos(angles))

def attend(queries, key_rows, value_rows, head_count):
    query_count = queries.shape[0]
    head_size = queries.shape[1] // head_count
    query_heads = queries.astype(jnp.float32).reshape(query_count, head_count, head_size)
    key_heads = key_rows.astype(jnp.float32).reshape(key_rows.shape[0], head_count, head_size)
    value_heads = value_rows.astype(jnp.float32).reshape(value_rows.shape[0], head_count, head_size)
    scores = jnp.einsum('qhd,khd->hqk', query_heads, key_heads) / math.sqrt(head_size)
    raised = jnp.exp(scores - lax.optimization_barrier(jnp.max(scores, axis=-1, keepdims=True)))
    totals = lax.optimization_barrier(jnp.sum(raised, axis=-1))
    weights = lax.optimization_barrier(raised.astype(jnp.bfloat16)).astype(jnp.float32)
    context = jnp.einsum('hqk,khd->qhd', weights, value_heads) / jnp.transpose(totals)[:, :, None]
    return context.reshape(query_count, head_count * head_size).astype(jnp.bfloat16)

def reference(vis_tokens, vis_counts, vis_spatial, enc_gain, enc_bias, enc_qkv, enc_proj, final_gain, final_bias, to_decoder, mask_token, dec_gain, dec_bias, dec_qkv):
    visible = jnp.arange(VIS, dtype=jnp.int32)
    position_table = sinusoid(jnp.arange(L, dtype=jnp.int32), DD)
    outputs = []
    for clip_index in range(CLIPS):
        counts = vis_counts[clip_index]
        member_ends = jnp.cumsum(counts)
        starts = member_ends - counts
        member = lax.optimization_barrier(jnp.sum((visible[:, None] >= member_ends[None, :]).astype(jnp.int32), axis=1))
        slot_index = visible - starts[member]
        token_rows = vis_tokens[(member * CLIPS + clip_index) * VCAP + slot_index].astype(jnp.float32)
        normed = layer_norm(token_rows, enc_gain, enc_bias).astype(jnp.bfloat16)
        enc_query = jnp.dot(normed, enc_qkv[0], preferred_element_type=jnp.float32).astype(jnp.bfloat16)
        enc_key = jnp.dot(normed, enc_qkv[1], preferred_element_type=jnp.float32).astype(jnp.bfloat16)
        enc_value = jnp.dot(normed, enc_qkv[2], preferred_element_type=jnp.float32).astype(jnp.bfloat16)
        context = attend(enc_query, enc_key, enc_value, HEADS)
        residual = token_rows + jnp.dot(context, enc_proj, preferred_element_type=jnp.float32)
        final_rows = layer_norm(residual, final_gain, final_bias).astype(jnp.bfloat16)
        encoded = jnp.dot(final_rows, to_decoder, preferred_element_type=jnp.float32).astype(jnp.bfloat16)
        position = visible // VSP * S + vis_spatial[clip_index][visible % VSP]
        filled = jnp.broadcast_to(mask_token, (L, DD)).at[position].set(encoded.astype(jnp.float32))
        inputs = position_table + filled
        dec_normed = layer_norm(inputs, dec_gain, dec_bias).astype(jnp.bfloat16)
        dec_query = jnp.dot(dec_normed, dec_qkv[0], preferred_element_type=jnp.float32).astype(jnp.bfloat16)
        dec_key = jnp.dot(dec_normed, dec_qkv[1], preferred_element_type=jnp.float32).astype(jnp.bfloat16)
        dec_value = jnp.dot(dec_normed, dec_qkv[2], preferred_element_type=jnp.float32).astype(jnp.bfloat16)
        query_blocks = dec_query.reshape(ROUNDS, L // ROUNDS, DD)
        decoded = lax.map(lambda query_block: attend(query_block, dec_key, dec_value, DHEADS), query_blocks)
        outputs.append(decoded)
    return jnp.stack(outputs)
```

```python
import math

import jax
import jax.numpy as jnp
from jax import lax
from jax.experimental import pallas as pl
from jax.experimental.pallas import tpu as pltpu
from jax.sharding import PartitionSpec as P

D = 1408
HEADS = 16
DD = 512
DHEADS = 8
S = 1024
BLOCK = 32
VB = 3
GROUP = 8
L = 16384
VSP = 96
VIS = 1536
FRAMES = L // S
CLIPS = 4
SLOTS = 384
QUARTER = 96
CHUNK = 128
CHUNKS = S // CHUNK
KEYS = CHUNK * FRAMES
OWN = FRAMES * BLOCK
OWNVIS = FRAMES * VB
HEAD = DD // DHEADS
LOG2E = 1.4426950408889634
epsilon = 1e-06
floor_score = -1e30
NT = (((1,), (1,)), ((), ()))


def layer_norm(values, gain_row, bias_row):
    centre = jnp.mean(values, axis=-1, keepdims=True)
    centred = values - centre
    spread = jnp.mean(centred * centred, axis=-1, keepdims=True)
    return centred * lax.rsqrt(spread + epsilon) * gain_row + bias_row


def frequencies():
    column_ids = jnp.arange(DD, dtype=jnp.int32)
    exponent = (2 * (column_ids // 2)).astype(jnp.float32) / DD
    return column_ids % 2 == 0, jnp.exp(exponent * -math.log(10000.0))


def sinusoid(positions):
    even, frequency = frequencies()
    angles = positions.astype(jnp.float32)[:, None] * frequency[None, :]
    return jnp.where(even[None, :], jnp.sin(angles), jnp.cos(angles))


TILES = 8


def table_kernel(a1, a2, b1, b2, token, gain, bias, wkv, keep, k_ref, v_ref):
    lanes = lax.broadcasted_iota(jnp.int32, (1, 2 * HEAD), 1)
    for tile in range(TILES):
        rows = pl.ds(tile * CHUNK, CHUNK)
        x = a1[0, tile : tile + 1, :] * b1[...] + a2[0, tile : tile + 1, :] * b2[...] + token[...]
        h = layer_norm(x, gain[...], bias[...]).astype(jnp.bfloat16)
        kv = jnp.dot(h, wkv[...], preferred_element_type=jnp.float32)
        k_ref[rows, :] = kv[:, : 2 * HEAD].astype(jnp.bfloat16)
        v = kv[:, 2 * HEAD :]
        turned = pltpu.roll(v, HEAD, 1)
        for head in range(2):
            twice = jnp.where((lanes < HEAD) == (head == 0), v, turned)
            v_ref[head, rows, :] = (jnp.concatenate([twice, twice], axis=1) * keep[0]).astype(jnp.bfloat16)


def angle_tables(coarse, fine):
    even, frequency = frequencies()
    angle_a = coarse.astype(jnp.float32)[:, None] * frequency[None, :]
    angle_b = fine.astype(jnp.float32)[:, None] * frequency[None, :]
    sin_a, cos_a = jnp.sin(angle_a), jnp.cos(angle_a)
    a1 = jnp.where(even[None, :], sin_a, cos_a)
    a2 = jnp.where(even[None, :], cos_a, -sin_a)
    return lax.optimization_barrier((a1, a2, jnp.cos(angle_b), jnp.sin(angle_b)))


def make_tables(mask_token, dec_gain, dec_bias, wkv, keep):
    coarse = (jnp.arange(FRAMES) * S)[None, :] + (jnp.arange(CHUNKS) * CHUNK)[:, None]
    a1, a2, b1, b2 = angle_tables(coarse.reshape(-1), jnp.arange(CHUNK))
    a1, a2 = a1.reshape(-1, TILES, DD), a2.reshape(-1, TILES, DD)
    steps = a1.shape[0]
    per_chunk = steps // CHUNKS
    whole = lambda *shape: pl.BlockSpec(shape, lambda i: (0,) * len(shape))
    return pl.pallas_call(
        table_kernel,
        grid=(steps,),
        in_specs=[
            pl.BlockSpec((1, TILES, DD), lambda i: (i, 0, 0)),
            pl.BlockSpec((1, TILES, DD), lambda i: (i, 0, 0)),
            whole(CHUNK, DD),
            whole(CHUNK, DD),
            whole(1, DD),
            whole(1, DD),
            whole(1, DD),
            whole(DD, 4 * HEAD),
            pl.BlockSpec((1, CHUNK, CLIPS * HEAD), lambda i: (i // per_chunk, 0, 0)),
        ],
        out_specs=[
            pl.BlockSpec((TILES * CHUNK, 2 * HEAD), lambda i: (i, 0)),
            pl.BlockSpec((2, TILES * CHUNK, CLIPS * HEAD), lambda i: (0, i, 0)),
        ],
        out_shape=[
            jax.ShapeDtypeStruct((L, 2 * HEAD), jnp.bfloat16),
            jax.ShapeDtypeStruct((2, L, CLIPS * HEAD), jnp.bfloat16),
        ],
        cost_estimate=pl.CostEstimate(flops=20 * 10**9, bytes_accessed=25 * 10**6, transcendentals=0),
        name="masked_tables",
    )(a1, a2, b1, b2, mask_token[None], dec_gain[None], dec_bias[None], wkv, keep)


def lane_tiles(x):
    total = x[:, :CHUNK]
    for tile in range(1, x.shape[1] // CHUNK):
        total = total + x[:, tile * CHUNK : (tile + 1) * CHUNK]
    return total


BASE_ROWS = 128
JOIN_ROWS = 512


def base_kernel(q_ref, k_ref, v_ref, keep_ref, acc_ref, m_ref, l_ref):
    first = pl.program_id(1) == 0

    @pl.when(first)
    def _():
        acc_ref[...] = jnp.zeros_like(acc_ref)
        l_ref[...] = jnp.zeros_like(l_ref)
        m_ref[...] = jnp.full_like(m_ref, floor_score)

    for start in range(0, OWN, BASE_ROWS):
        rows = pl.ds(start, BASE_ROWS)
        s = lax.dot_general(q_ref[0, rows, :], k_ref[...], NT, preferred_element_type=jnp.float32)
        old = m_ref[0, rows, :]
        new = jnp.maximum(old, jnp.max(s, axis=1, keepdims=True))
        factor = jnp.exp2((old - new) * LOG2E)
        e = jnp.exp2((s - new[:, :1]) * LOG2E)
        total = lane_tiles(e)
        for clip in range(CLIPS):
            l_ref[0, clip, rows, :] = l_ref[0, clip, rows, :] * factor + total * keep_ref[0, clip : clip + 1, :]
        m_ref[0, rows, :] = new
        update = jnp.dot(e.astype(jnp.bfloat16), v_ref[0], preferred_element_type=jnp.float32)
        acc_ref[0, rows, :] = acc_ref[0, rows, :] * jnp.concatenate([factor, factor], axis=1) + update


def base_attention(q, k, v4, keep_rows):
    return pl.pallas_call(
        base_kernel,
        grid=(2, CHUNKS),
        in_specs=[
            pl.BlockSpec((1, OWN, 2 * HEAD), lambda h, j: (h, 0, 0)),
            pl.BlockSpec((KEYS, 2 * HEAD), lambda h, j: (j, 0)),
            pl.BlockSpec((1, KEYS, CLIPS * HEAD), lambda h, j: (h, j, 0)),
            pl.BlockSpec((1, CLIPS, CHUNK), lambda h, j: (j, 0, 0)),
        ],
        out_specs=[
            pl.BlockSpec((1, OWN, CLIPS * HEAD), lambda h, j: (h, 0, 0)),
            pl.BlockSpec((1, OWN, CHUNK), lambda h, j: (h, 0, 0)),
            pl.BlockSpec((1, CLIPS, OWN, CHUNK), lambda h, j: (h, 0, 0, 0)),
        ],
        out_shape=[
            jax.ShapeDtypeStruct((2, OWN, CLIPS * HEAD), jnp.float32),
            jax.ShapeDtypeStruct((2, OWN, CHUNK), jnp.float32),
            jax.ShapeDtypeStruct((2, CLIPS, OWN, CHUNK), jnp.float32),
        ],
        cost_estimate=pl.CostEstimate(flops=25 * 10**9, bytes_accessed=25 * 10**6, transcendentals=17 * 10**6),
        name="masked_queries",
    )(q, k, v4, keep_rows)


def single_kernel(q_ref, k_ref, v_ref, offset_ref, acc_ref, m_ref, l_ref):
    @pl.when(pl.program_id(1) == 0)
    def _():
        acc_ref[...] = jnp.zeros_like(acc_ref)
        l_ref[...] = jnp.zeros_like(l_ref)
        m_ref[...] = jnp.full_like(m_ref, floor_score)

    offset = jnp.concatenate([offset_ref[0]] * FRAMES, axis=1)
    for head in range(2):
        s = lax.dot_general(q_ref[head], k_ref[...], NT, preferred_element_type=jnp.float32) + offset
        old = m_ref[head]
        new = jnp.maximum(old, jnp.max(s, axis=1, keepdims=True))
        factor = jnp.exp2((old - new) * LOG2E)
        e = jnp.exp2((s - new[:, :1]) * LOG2E)
        l_ref[head] = l_ref[head] * factor + lane_tiles(e)
        m_ref[head] = new
        update = jnp.dot(e.astype(jnp.bfloat16), v_ref[head], preferred_element_type=jnp.float32)
        acc_ref[head] = acc_ref[head] * jnp.concatenate([factor, factor], axis=1) + update


def single_attention(q, k, v4, offsets, block):
    rows = q.shape[1]
    blocks = rows // block
    offset_map = (lambda r, j: (j, r, 0)) if offsets.shape[1] == rows else (lambda r, j: (j, 0, 0))
    out_spec = lambda width: pl.BlockSpec((2, block, width), lambda r, j: (0, r, 0))
    return pl.pallas_call(
        single_kernel,
        grid=(blocks, CHUNKS),
        in_specs=[
            pl.BlockSpec((2, block, 2 * HEAD), lambda r, j: (0, r, 0)),
            pl.BlockSpec((KEYS, 2 * HEAD), lambda r, j: (j, 0)),
            pl.BlockSpec((2, KEYS, CLIPS * HEAD), lambda r, j: (0, j, 0)),
            pl.BlockSpec((1, block, CHUNK), offset_map),
        ],
        out_specs=[out_spec(CLIPS * HEAD), out_spec(CHUNK), out_spec(CHUNK)],
        out_shape=[
            jax.ShapeDtypeStruct((2, rows, CLIPS * HEAD), jnp.float32),
            jax.ShapeDtypeStruct((2, rows, CHUNK), jnp.float32),
            jax.ShapeDtypeStruct((2, rows, CHUNK), jnp.float32),
        ],
        cost_estimate=pl.CostEstimate(flops=20 * 10**9, bytes_accessed=25 * 10**6, transcendentals=6 * 10**6),
        name="visible_queries" if blocks == 1 else "masked_queries_by_clip",
    )(q, k, v4, offsets)


def own_columns(acc, clip, head):
    piece = jnp.where(clip >= 2, acc[:, CHUNK:], acc[:, :CHUNK])
    return jnp.where(clip % 2 == head, piece, pltpu.roll(piece, HEAD, 1))


def join(q, k, v, acc, m, l):
    s = lax.dot_general(q, k, NT, preferred_element_type=jnp.float32)
    new = jnp.maximum(m, jnp.max(s, axis=1, keepdims=True))
    e = jnp.exp2((s - new[:, :1]) * LOG2E)
    factor = jnp.exp2((m - new) * LOG2E)
    total = jnp.sum(l * factor + lane_tiles(e), axis=1, keepdims=True)
    update = jnp.dot(e.astype(jnp.bfloat16), v, preferred_element_type=jnp.float32)
    return (acc * factor + update) / total


def join_kernel(qb_ref, qv_ref, kv_ref, accb_ref, mb_ref, lb_ref, accv_ref, mv_ref, lv_ref, place_ref, out_ref):
    clip = pl.program_id(0)
    lanes = lax.broadcasted_iota(jnp.int32, (1, 2 * HEAD), 1)
    k = kv_ref[:, 0, :, : 2 * HEAD].reshape(VIS, 2 * HEAD)
    v = kv_ref[:, 0, :, 2 * HEAD :].reshape(VIS, 2 * HEAD)
    place = place_ref[0]
    seen = jnp.sum(place, axis=1, keepdims=True) > 0.5
    for head in range(2):
        mine = (lanes // HEAD) == head
        vis = join(
            qv_ref[head, 0], k, v, own_columns(accv_ref[head, 0], clip, head), mv_ref[head, 0], lv_ref[head, 0]
        ).astype(jnp.bfloat16)
        for start in range(0, OWN, JOIN_ROWS):
            rows = pl.ds(start, JOIN_ROWS)
            base = join(
                qb_ref[head, rows, :],
                k,
                v,
                own_columns(accb_ref[head, rows, :], clip, head),
                mb_ref[head, 0, rows, :],
                lb_ref[head, 0, rows, :],
            )
            spread = jnp.dot(
                place[start : start + JOIN_ROWS].astype(jnp.bfloat16), vis, preferred_element_type=jnp.float32
            )
            value = jnp.where(seen[start : start + JOIN_ROWS], spread, base).astype(jnp.bfloat16)
            if head == 0:
                out_ref[0, rows, :] = value
            else:
                out_ref[0, rows, :] = jnp.where(mine, value, out_ref[0, rows, :])


def join_attention(qb, qv, kv, base, single, place):
    seq_count = kv.shape[0]
    accb, mb, lb = base
    accv, mv, lv = [x.reshape(2, CLIPS, OWNVIS, -1) for x in single]
    vis_spec = lambda width: pl.BlockSpec((2, 1, OWNVIS, width), lambda c: (0, c, 0, 0))
    return pl.pallas_call(
        join_kernel,
        grid=(CLIPS,),
        in_specs=[
            pl.BlockSpec((2, OWN, 2 * HEAD), lambda c: (0, 0, 0)),
            vis_spec(2 * HEAD),
            pl.BlockSpec((seq_count, 1, OWNVIS, 4 * HEAD), lambda c: (0, c, 0, 0)),
            pl.BlockSpec((2, OWN, CLIPS * HEAD), lambda c: (0, 0, 0)),
            pl.BlockSpec((2, 1, OWN, CHUNK), lambda c: (0, c, 0, 0)),
            pl.BlockSpec((2, 1, OWN, CHUNK), lambda c: (0, c, 0, 0)),
            vis_spec(CLIPS * HEAD),
            vis_spec(CHUNK),
            vis_spec(CHUNK),
            pl.BlockSpec((1, OWN, OWNVIS), lambda c: (c, 0, 0)),
        ],
        out_specs=pl.BlockSpec((1, OWN, 2 * HEAD), lambda c: (c, 0, 0)),
        out_shape=jax.ShapeDtypeStruct((CLIPS, OWN, 2 * HEAD), jnp.bfloat16),
        cost_estimate=pl.CostEstimate(flops=8 * 10**9, bytes_accessed=10**7, transcendentals=7 * 10**6),
        name="join_visible_keys",
    )(qb, qv.reshape(2, CLIPS, OWNVIS, -1), kv, accb, mb, lb, accv, mv, lv, place)


def project_kernel(x_ref, gain_ref, bias_ref, w_ref, q_ref, kv_ref, h_ref):
    part = pl.program_id(0)

    @pl.when(part == 0)
    def _():
        h_ref[...] = layer_norm(x_ref[...].astype(jnp.float32), gain_ref[...], bias_ref[...]).astype(jnp.bfloat16)

    value = lax.dot_general(h_ref[...], w_ref[0], NT, preferred_element_type=jnp.float32).astype(jnp.bfloat16)

    @pl.when(part == 2)
    def _():
        q_ref[...] = value

    @pl.when(part < 2)
    def _():
        kv_ref[0] = value


def encoder_projections(x, gain, bias, w):
    slots, width = x.shape[0], w.shape[1]
    return pl.pallas_call(
        project_kernel,
        grid=(3,),
        in_specs=[
            pl.BlockSpec((slots, D), lambda i: (0, 0)),
            pl.BlockSpec((1, D), lambda i: (0, 0)),
            pl.BlockSpec((1, D), lambda i: (0, 0)),
            pl.BlockSpec((1, width, D), lambda i: ((i + 1) % 3, 0, 0)),
        ],
        out_specs=[
            pl.BlockSpec((slots, width), lambda i: (0, 0)),
            pl.BlockSpec((1, slots, width), lambda i: (jnp.minimum(i, 1), 0, 0)),
        ],
        out_shape=[
            jax.ShapeDtypeStruct((slots, width), jnp.bfloat16),
            jax.ShapeDtypeStruct((2, slots, width), jnp.bfloat16),
        ],
        scratch_shapes=[pltpu.VMEM((slots, D), jnp.bfloat16)],
        cost_estimate=pl.CostEstimate(flops=12 * 10**8, bytes_accessed=5 * 10**6, transcendentals=0),
        name="encoder_projections",
    )(x, gain[None], bias[None], w)


def encoder_kernel(q_ref, kv_ref, offset_ref, out_ref):
    width = q_ref.shape[1]
    head_size = D // HEADS
    k = kv_ref[:, 0].reshape(GROUP * SLOTS, width)
    v = kv_ref[:, 1].reshape(GROUP * SLOTS, width)
    scale = LOG2E / math.sqrt(head_size)
    sums = []
    for low, high, heads in ((0, 256, (0, 1)), (128, width, (2, 3))):
        lanes = lax.broadcasted_iota(jnp.int32, (1, high - low), 1) + low
        window = q_ref[:, low:high]
        result = None
        for head in heads:
            mine = (lanes >= head * head_size) & (lanes < (head + 1) * head_size)
            q = jnp.where(mine, window, jnp.zeros_like(window))
            s = lax.dot_general(q, k[:, low:high], NT, preferred_element_type=jnp.float32) * scale + offset_ref[...]
            e = jnp.exp2(s - jnp.max(s, axis=1, keepdims=True))
            total = jnp.sum(lane_tiles(e), axis=1, keepdims=True)
            context = jnp.dot(e.astype(jnp.bfloat16), v[:, low:high], preferred_element_type=jnp.float32)
            context = jnp.where(mine, context / total, 0.0)
            result = context if result is None else result + context
        sums.append(result)
    out_ref[:, :128] = sums[0][:, :128].astype(jnp.bfloat16)
    out_ref[:, 128:256] = (sums[0][:, 128:] + sums[1][:, :128]).astype(jnp.bfloat16)
    out_ref[:, 256:] = sums[1][:, 128:].astype(jnp.bfloat16)


def encoder_attention(q, kv, offset):
    return pl.pallas_call(
        encoder_kernel,
        in_specs=[pl.BlockSpec(memory_space=pltpu.VMEM)] * 3,
        out_specs=pl.BlockSpec(memory_space=pltpu.VMEM),
        out_shape=jax.ShapeDtypeStruct(q.shape, jnp.bfloat16),
        cost_estimate=pl.CostEstimate(flops=9 * 10**9, bytes_accessed=5 * 10**6, transcendentals=5 * 10**6),
        name="encoder_attention",
    )(q, kv, offset)


def body(
    vis_tokens,
    vis_counts,
    vis_spatial,
    enc_gain,
    enc_bias,
    enc_qkv,
    enc_proj,
    final_gain,
    final_bias,
    to_decoder,
    mask_token,
    dec_gain,
    dec_bias,
    dec_qkv,
):
    seq_count = lax.axis_size("seq")
    seq_index = lax.axis_index("seq")
    quarter = lax.axis_index("head")
    clip_index = seq_index % CLIPS
    member = seq_index // CLIPS
    slot_ids = jnp.arange(SLOTS, dtype=jnp.int32)
    starts = jnp.cumsum(vis_counts, axis=1) - vis_counts
    group_counts = lax.dynamic_index_in_dim(vis_counts, clip_index, 0, keepdims=False)
    before = lax.dynamic_slice(starts, (clip_index, member), (1, 1))[0, 0]

    enc_q, enc_kv = encoder_projections(vis_tokens, enc_gain, enc_bias, jnp.swapaxes(enc_qkv, 1, 2))
    groups = [[clip + CLIPS * g for g in range(GROUP)] for clip in range(CLIPS)]
    group_kv = lax.all_gather(enc_kv, "seq", axis_index_groups=groups)
    live = (slot_ids[None, :] < group_counts[:, None]).reshape(1, GROUP * SLOTS)

    frame_ids = jnp.arange(S, dtype=jnp.int32)
    flags = jnp.any(vis_spatial[:, :, None] == frame_ids[None, None, :], axis=1)
    kept = jnp.where(flags, 0.0, 1.0)
    keep_rows = kept.reshape(CLIPS, CHUNKS, CHUNK).transpose(1, 0, 2)
    lane_clip = jnp.arange(CLIPS * HEAD, dtype=jnp.int32) // HEAD
    clip_lanes = (lane_clip[None, :] == jnp.arange(CLIPS)[:, None]).astype(jnp.float32)
    keep = jnp.dot(kept.T, clip_lanes, precision=lax.Precision.HIGHEST).reshape(CHUNKS, CHUNK, CLIPS * HEAD)
    offset_rows = (1.0 - keep_rows) * floor_score
    offsets = jnp.repeat(offset_rows, OWNVIS, axis=1)
    wkv = jnp.concatenate([dec_qkv[1], dec_qkv[2]], axis=1)
    k_masked, v_masked = make_tables(mask_token, dec_gain, dec_bias, wkv, keep)

    own_ids = jnp.arange(OWN, dtype=jnp.int32)
    own_frame, own_place = own_ids // BLOCK, own_ids % BLOCK
    scale = 1.0 / math.sqrt(HEAD)
    head_of_lane = jnp.arange(2 * HEAD, dtype=jnp.int32) // HEAD

    def split_heads(q):
        q = (q.astype(jnp.bfloat16) * jnp.bfloat16(scale))[None]
        return jnp.where(jnp.arange(2)[:, None, None] == head_of_lane[None, None, :], q, jnp.bfloat16(0))

    own_spatial = lax.dynamic_slice(vis_spatial, (0, seq_index * VB), (CLIPS, VB))
    fine = jnp.concatenate([seq_index * BLOCK + jnp.arange(BLOCK, dtype=jnp.int32), own_spatial.reshape(-1)])
    a1, a2, b1, b2 = angle_tables(jnp.arange(FRAMES, dtype=jnp.int32) * S, fine)
    own_table = a1[:, None, :] * b1[None, :BLOCK] + a2[:, None, :] * b2[None, :BLOCK]
    own_table = own_table.reshape(OWN, DD) + mask_token[None, :]
    base_in = layer_norm(own_table, dec_gain, dec_bias).astype(jnp.bfloat16)
    q_masked = split_heads(jnp.dot(base_in, dec_qkv[0], preferred_element_type=jnp.float32))
    b1, b2 = b1[BLOCK:].reshape(CLIPS, 1, VB, DD), b2[BLOCK:].reshape(CLIPS, 1, VB, DD)
    vis_table = a1[None, :, None, :] * b1 + a2[None, :, None, :] * b2
    base = base_attention(q_masked, k_masked, v_masked, keep_rows)
    source = (slot_ids - before) % SLOTS
    turn = (source[:, None] == slot_ids[None, :]).astype(jnp.bfloat16)
    turn_part = lax.dynamic_slice_in_dim(turn, quarter * QUARTER, QUARTER, 0)
    tokens_part = jnp.dot(turn_part, vis_tokens, preferred_element_type=jnp.float32)
    group_kv, base, tokens_part, vis_table, turn = lax.optimization_barrier(
        (group_kv, base, tokens_part, vis_table, turn)
    )

    def by_clip(_):
        offset = jnp.broadcast_to(
            offset_rows.transpose(1, 0, 2)[:, :, None, :], (CLIPS, CHUNKS, BASE_ROWS, CHUNK)
        )
        accs, ms, ls = lax.map(lambda x: single_attention(q_masked, k_masked, v_masked, x, BASE_ROWS), offset)
        acc = accs[0]
        for clip in range(1, CLIPS):
            acc = jnp.where(lane_clip[None, None, :] == clip, accs[clip], acc)
        return acc, jnp.swapaxes(ms, 0, 1), jnp.swapaxes(ls, 0, 1)

    def shared(_):
        return base[0], jnp.broadcast_to(base[1][:, None], (2, CLIPS, OWN, CHUNK)), base[2]

    vanishing = jnp.min(jnp.sum(base[2], axis=-1)) < 2.0**-60
    base = lax.cond(vanishing, by_clip, shared, None)

    context = encoder_attention(enc_q, group_kv, jnp.where(live, 0.0, floor_score))
    turned = jnp.dot(turn, context, preferred_element_type=jnp.float32).astype(jnp.bfloat16)
    partial_out = jnp.dot(turned, enc_proj, preferred_element_type=jnp.float32).astype(jnp.bfloat16)
    attended = lax.psum_scatter(partial_out, "head", scatter_dimension=0, tiled=True).astype(jnp.float32)
    final_rows = layer_norm(tokens_part + attended, final_gain, final_bias).astype(jnp.bfloat16)
    encoded = jnp.dot(final_rows, to_decoder, preferred_element_type=jnp.float32).astype(jnp.bfloat16)

    arrived = lax.all_to_all(encoded.reshape(seq_count, VB, DD), "seq", split_axis=0, concat_axis=0, tiled=True)
    arrived = lax.all_gather(arrived, "head")
    a_ids = jnp.arange(4, dtype=jnp.int32)[:, None, None]
    from_ids = jnp.arange(seq_count, dtype=jnp.int32)
    i_ids = jnp.arange(VB, dtype=jnp.int32)[None, None, :]
    from_start = starts.T.reshape(-1)[None, :, None]
    from_count = vis_counts.T.reshape(-1)[None, :, None]
    row = a_ids * VSP + seq_index * VB + i_ids
    offset_in = (row - from_start) % SLOTS
    token = from_start + offset_in
    frame = token // VSP
    target = (from_ids % CLIPS)[None, :, None] * OWNVIS + frame * VB + i_ids
    target = jnp.where(offset_in < from_count, target, -1).reshape(-1)
    pick = (jnp.arange(CLIPS * OWNVIS, dtype=jnp.int32)[:, None] == target[None, :]).astype(jnp.bfloat16)
    own_encoded = jnp.dot(pick, arrived.reshape(-1, DD), preferred_element_type=jnp.float32)

    vis_in = vis_table.reshape(CLIPS * OWNVIS, DD) + own_encoded
    vis_in = layer_norm(vis_in, dec_gain, dec_bias).astype(jnp.bfloat16)
    vis_q, vis_k, vis_v = [jnp.dot(vis_in, dec_qkv[i], preferred_element_type=jnp.float32) for i in range(3)]
    vis_kv = jnp.concatenate([vis_k, vis_v], axis=1).astype(jnp.bfloat16).reshape(CLIPS, OWNVIS, 4 * HEAD)
    all_kv = lax.all_gather(vis_kv, "seq")
    q_visible = split_heads(vis_q)
    single = single_attention(q_visible, k_masked, v_masked, offsets, CLIPS * OWNVIS)

    token_ids = jnp.arange(OWNVIS, dtype=jnp.int32)
    token_place = jnp.repeat(own_spatial[:, None, :] - seq_index * BLOCK, FRAMES, axis=1).reshape(CLIPS, 1, OWNVIS)
    place = (own_frame[None, :, None] == (token_ids // VB)[None, None, :]) & (own_place[None, :, None] == token_place)
    place = place.astype(jnp.float32)

    out = join_attention(q_masked, q_visible, all_kv, base, single, place)
    return out.reshape(CLIPS, FRAMES, BLOCK, 2 * HEAD)


def solution(mesh):
    in_specs = (
        P("seq", None),
        P(),
        P(),
        P(),
        P(),
        P(None, None, "head"),
        P("head", None),
        P(),
        P(),
        P(),
        P(),
        P(),
        P(),
        P(None, None, "head"),
    )
    out_specs = P(None, None, "seq", "head")
    return jax.shard_map(body, mesh=mesh, in_specs=in_specs, out_specs=out_specs, check_vma=False)
```

```python
import math

import jax
import jax.numpy as jnp
from jax import lax
from jax.experimental import pallas as pl
from jax.experimental.pallas import tpu as pltpu
from jax.sharding import PartitionSpec as P

D = 1408
HEADS = 16
DD = 512
DHEADS = 8
S = 1024
BLOCK = 32
VB = 3
GROUP = 8
L = 16384
VSP = 96
VIS = 1536
FRAMES = L // S
CLIPS = 4
SLOTS = 384
QUARTER = 96
CHUNK = 128
CHUNKS = S // CHUNK
KEYS = CHUNK * FRAMES
OWN = FRAMES * BLOCK
OWNVIS = FRAMES * VB
HEAD = DD // DHEADS
LOG2E = 1.4426950408889634
epsilon = 1e-06
floor_score = -1e30
NT = (((1,), (1,)), ((), ()))


def layer_norm(values, gain_row, bias_row):
    centre = jnp.mean(values, axis=-1, keepdims=True)
    centred = values - centre
    spread = jnp.mean(centred * centred, axis=-1, keepdims=True)
    return centred * lax.rsqrt(spread + epsilon) * gain_row + bias_row


def frequencies():
    column_ids = jnp.arange(DD, dtype=jnp.int32)
    exponent = (2 * (column_ids // 2)).astype(jnp.float32) / DD
    return column_ids % 2 == 0, jnp.exp(exponent * -math.log(10000.0))


def sinusoid(positions):
    even, frequency = frequencies()
    angles = positions.astype(jnp.float32)[:, None] * frequency[None, :]
    return jnp.where(even[None, :], jnp.sin(angles), jnp.cos(angles))


TILES = 8


def table_kernel(a1, a2, b1, b2, token, gain, bias, wkv, keep, k_ref, v_ref):
    lanes = lax.broadcasted_iota(jnp.int32, (1, 2 * HEAD), 1)
    for tile in range(TILES):
        rows = pl.ds(tile * CHUNK, CHUNK)
        x = a1[0, tile : tile + 1, :] * b1[...] + a2[0, tile : tile + 1, :] * b2[...] + token[...]
        h = layer_norm(x, gain[...], bias[...]).astype(jnp.bfloat16)
        kv = jnp.dot(h, wkv[...], preferred_element_type=jnp.float32)
        k_ref[rows, :] = kv[:, : 2 * HEAD].astype(jnp.bfloat16)
        v = kv[:, 2 * HEAD :]
        turned = pltpu.roll(v, HEAD, 1)
        for head in range(2):
            twice = jnp.where((lanes < HEAD) == (head == 0), v, turned)
            v_ref[head, rows, :] = (jnp.concatenate([twice, twice], axis=1) * keep[0]).astype(jnp.bfloat16)


def angle_tables(coarse, fine):
    even, frequency = frequencies()
    angle_a = coarse.astype(jnp.float32)[:, None] * frequency[None, :]
    angle_b = fine.astype(jnp.float32)[:, None] * frequency[None, :]
    sin_a, cos_a = jnp.sin(angle_a), jnp.cos(angle_a)
    a1 = jnp.where(even[None, :], sin_a, cos_a)
    a2 = jnp.where(even[None, :], cos_a, -sin_a)
    return lax.optimization_barrier((a1, a2, jnp.cos(angle_b), jnp.sin(angle_b)))


def make_tables(mask_token, dec_gain, dec_bias, wkv, keep):
    coarse = (jnp.arange(FRAMES) * S)[None, :] + (jnp.arange(CHUNKS) * CHUNK)[:, None]
    a1, a2, b1, b2 = angle_tables(coarse.reshape(-1), jnp.arange(CHUNK))
    a1, a2 = a1.reshape(-1, TILES, DD), a2.reshape(-1, TILES, DD)
    steps = a1.shape[0]
    per_chunk = steps // CHUNKS
    whole = lambda *shape: pl.BlockSpec(shape, lambda i: (0,) * len(shape))
    return pl.pallas_call(
        table_kernel,
        grid=(steps,),
        in_specs=[
            pl.BlockSpec((1, TILES, DD), lambda i: (i, 0, 0)),
            pl.BlockSpec((1, TILES, DD), lambda i: (i, 0, 0)),
            whole(CHUNK, DD),
            whole(CHUNK, DD),
            whole(1, DD),
            whole(1, DD),
            whole(1, DD),
            whole(DD, 4 * HEAD),
            pl.BlockSpec((1, CHUNK, CLIPS * HEAD), lambda i: (i // per_chunk, 0, 0)),
        ],
        out_specs=[
            pl.BlockSpec((TILES * CHUNK, 2 * HEAD), lambda i: (i, 0)),
            pl.BlockSpec((2, TILES * CHUNK, CLIPS * HEAD), lambda i: (0, i, 0)),
        ],
        out_shape=[
            jax.ShapeDtypeStruct((L, 2 * HEAD), jnp.bfloat16),
            jax.ShapeDtypeStruct((2, L, CLIPS * HEAD), jnp.bfloat16),
        ],
        cost_estimate=pl.CostEstimate(flops=20 * 10**9, bytes_accessed=25 * 10**6, transcendentals=0),
        name="masked_tables",
    )(a1, a2, b1, b2, mask_token[None], dec_gain[None], dec_bias[None], wkv, keep)


def lane_tiles(x):
    total = x[:, :CHUNK]
    for tile in range(1, x.shape[1] // CHUNK):
        total = total + x[:, tile * CHUNK : (tile + 1) * CHUNK]
    return total


BASE_ROWS = 128
JOIN_ROWS = 512


def base_kernel(q_ref, k_ref, v_ref, keep_ref, acc_ref, m_ref, l_ref):
    first = pl.program_id(1) == 0

    @pl.when(first)
    def _():
        acc_ref[...] = jnp.zeros_like(acc_ref)
        l_ref[...] = jnp.zeros_like(l_ref)
        m_ref[...] = jnp.full_like(m_ref, floor_score)

    for start in range(0, OWN, BASE_ROWS):
        rows = pl.ds(start, BASE_ROWS)
        s = lax.dot_general(q_ref[0, rows, :], k_ref[...], NT, preferred_element_type=jnp.float32)
        old = m_ref[0, rows, :]
        new = jnp.maximum(old, jnp.max(s, axis=1, keepdims=True))
        factor = jnp.exp2((old - new) * LOG2E)
        e = jnp.exp2((s - new[:, :1]) * LOG2E)
        total = lane_tiles(e)
        for clip in range(CLIPS):
            l_ref[0, clip, rows, :] = l_ref[0, clip, rows, :] * factor + total * keep_ref[0, clip : clip + 1, :]
        m_ref[0, rows, :] = new
        update = jnp.dot(e.astype(jnp.bfloat16), v_ref[0], preferred_element_type=jnp.float32)
        acc_ref[0, rows, :] = acc_ref[0, rows, :] * jnp.concatenate([factor, factor], axis=1) + update


def base_attention(q, k, v4, keep_rows):
    return pl.pallas_call(
        base_kernel,
        grid=(2, CHUNKS),
        in_specs=[
            pl.BlockSpec((1, OWN, 2 * HEAD), lambda h, j: (h, 0, 0)),
            pl.BlockSpec((KEYS, 2 * HEAD), lambda h, j: (j, 0)),
            pl.BlockSpec((1, KEYS, CLIPS * HEAD), lambda h, j: (h, j, 0)),
            pl.BlockSpec((1, CLIPS, CHUNK), lambda h, j: (j, 0, 0)),
        ],
        out_specs=[
            pl.BlockSpec((1, OWN, CLIPS * HEAD), lambda h, j: (h, 0, 0)),
            pl.BlockSpec((1, OWN, CHUNK), lambda h, j: (h, 0, 0)),
            pl.BlockSpec((1, CLIPS, OWN, CHUNK), lambda h, j: (h, 0, 0, 0)),
        ],
        out_shape=[
            jax.ShapeDtypeStruct((2, OWN, CLIPS * HEAD), jnp.float32),
            jax.ShapeDtypeStruct((2, OWN, CHUNK), jnp.float32),
            jax.ShapeDtypeStruct((2, CLIPS, OWN, CHUNK), jnp.float32),
        ],
        cost_estimate=pl.CostEstimate(flops=25 * 10**9, bytes_accessed=25 * 10**6, transcendentals=17 * 10**6),
        name="masked_queries",
    )(q, k, v4, keep_rows)


def single_kernel(q_ref, k_ref, v_ref, offset_ref, acc_ref, m_ref, l_ref):
    @pl.when(pl.program_id(1) == 0)
    def _():
        acc_ref[...] = jnp.zeros_like(acc_ref)
        l_ref[...] = jnp.zeros_like(l_ref)
        m_ref[...] = jnp.full_like(m_ref, floor_score)

    offset = jnp.concatenate([offset_ref[0]] * FRAMES, axis=1)
    for head in range(2):
        s = lax.dot_general(q_ref[head], k_ref[...], NT, preferred_element_type=jnp.float32) + offset
        old = m_ref[head]
        new = jnp.maximum(old, jnp.max(s, axis=1, keepdims=True))
        factor = jnp.exp2((old - new) * LOG2E)
        e = jnp.exp2((s - new[:, :1]) * LOG2E)
        l_ref[head] = l_ref[head] * factor + lane_tiles(e)
        m_ref[head] = new
        update = jnp.dot(e.astype(jnp.bfloat16), v_ref[head], preferred_element_type=jnp.float32)
        acc_ref[head] = acc_ref[head] * jnp.concatenate([factor, factor], axis=1) + update


def single_attention(q, k, v4, offsets, block):
    rows = q.shape[1]
    blocks = rows // block
    offset_map = (lambda r, j: (j, r, 0)) if offsets.shape[1] == rows else (lambda r, j: (j, 0, 0))
    out_spec = lambda width: pl.BlockSpec((2, block, width), lambda r, j: (0, r, 0))
    return pl.pallas_call(
        single_kernel,
        grid=(blocks, CHUNKS),
        in_specs=[
            pl.BlockSpec((2, block, 2 * HEAD), lambda r, j: (0, r, 0)),
            pl.BlockSpec((KEYS, 2 * HEAD), lambda r, j: (j, 0)),
            pl.BlockSpec((2, KEYS, CLIPS * HEAD), lambda r, j: (0, j, 0)),
            pl.BlockSpec((1, block, CHUNK), offset_map),
        ],
        out_specs=[out_spec(CLIPS * HEAD), out_spec(CHUNK), out_spec(CHUNK)],
        out_shape=[
            jax.ShapeDtypeStruct((2, rows, CLIPS * HEAD), jnp.float32),
            jax.ShapeDtypeStruct((2, rows, CHUNK), jnp.float32),
            jax.ShapeDtypeStruct((2, rows, CHUNK), jnp.float32),
        ],
        cost_estimate=pl.CostEstimate(flops=20 * 10**9, bytes_accessed=25 * 10**6, transcendentals=6 * 10**6),
        name="visible_queries" if blocks == 1 else "masked_queries_by_clip",
    )(q, k, v4, offsets)


def own_columns(acc, clip, head):
    piece = jnp.where(clip >= 2, acc[:, CHUNK:], acc[:, :CHUNK])
    return jnp.where(clip % 2 == head, piece, pltpu.roll(piece, HEAD, 1))


def join(q, k, v, acc, m, l):
    s = lax.dot_general(q, k, NT, preferred_element_type=jnp.float32)
    new = jnp.maximum(m, jnp.max(s, axis=1, keepdims=True))
    e = jnp.exp2((s - new[:, :1]) * LOG2E)
    factor = jnp.exp2((m - new) * LOG2E)
    total = jnp.sum(l * factor + lane_tiles(e), axis=1, keepdims=True)
    update = jnp.dot(e.astype(jnp.bfloat16), v, preferred_element_type=jnp.float32)
    return (acc * factor + update) / total


def join_kernel(qb_ref, qv_ref, kv_ref, accb_ref, mb_ref, lb_ref, accv_ref, mv_ref, lv_ref, place_ref, out_ref):
    clip = pl.program_id(0)
    lanes = lax.broadcasted_iota(jnp.int32, (1, 2 * HEAD), 1)
    k = kv_ref[:, 0, :, : 2 * HEAD].reshape(VIS, 2 * HEAD)
    v = kv_ref[:, 0, :, 2 * HEAD :].reshape(VIS, 2 * HEAD)
    place = place_ref[0]
    seen = jnp.sum(place, axis=1, keepdims=True) > 0.5
    for head in range(2):
        mine = (lanes // HEAD) == head
        vis = join(
            qv_ref[head, 0], k, v, own_columns(accv_ref[head, 0], clip, head), mv_ref[head, 0], lv_ref[head, 0]
        ).astype(jnp.bfloat16)
        for start in range(0, OWN, JOIN_ROWS):
            rows = pl.ds(start, JOIN_ROWS)
            base = join(
                qb_ref[head, rows, :],
                k,
                v,
                own_columns(accb_ref[head, rows, :], clip, head),
                mb_ref[head, 0, rows, :],
                lb_ref[head, 0, rows, :],
            )
            spread = jnp.dot(
                place[start : start + JOIN_ROWS].astype(jnp.bfloat16), vis, preferred_element_type=jnp.float32
            )
            value = jnp.where(seen[start : start + JOIN_ROWS], spread, base).astype(jnp.bfloat16)
            if head == 0:
                out_ref[0, rows, :] = value
            else:
                out_ref[0, rows, :] = jnp.where(mine, value, out_ref[0, rows, :])


def join_attention(qb, qv, kv, base, single, place):
    seq_count = kv.shape[0]
    accb, mb, lb = base
    accv, mv, lv = [x.reshape(2, CLIPS, OWNVIS, -1) for x in single]
    vis_spec = lambda width: pl.BlockSpec((2, 1, OWNVIS, width), lambda c: (0, c, 0, 0))
    return pl.pallas_call(
        join_kernel,
        grid=(CLIPS,),
        in_specs=[
            pl.BlockSpec((2, OWN, 2 * HEAD), lambda c: (0, 0, 0)),
            vis_spec(2 * HEAD),
            pl.BlockSpec((seq_count, 1, OWNVIS, 4 * HEAD), lambda c: (0, c, 0, 0)),
            pl.BlockSpec((2, OWN, CLIPS * HEAD), lambda c: (0, 0, 0)),
            pl.BlockSpec((2, 1, OWN, CHUNK), lambda c: (0, c, 0, 0)),
            pl.BlockSpec((2, 1, OWN, CHUNK), lambda c: (0, c, 0, 0)),
            vis_spec(CLIPS * HEAD),
            vis_spec(CHUNK),
            vis_spec(CHUNK),
            pl.BlockSpec((1, OWN, OWNVIS), lambda c: (c, 0, 0)),
        ],
        out_specs=pl.BlockSpec((1, OWN, 2 * HEAD), lambda c: (c, 0, 0)),
        out_shape=jax.ShapeDtypeStruct((CLIPS, OWN, 2 * HEAD), jnp.bfloat16),
        cost_estimate=pl.CostEstimate(flops=8 * 10**9, bytes_accessed=10**7, transcendentals=7 * 10**6),
        name="join_visible_keys",
    )(qb, qv.reshape(2, CLIPS, OWNVIS, -1), kv, accb, mb, lb, accv, mv, lv, place)


def project_kernel(x_ref, gain_ref, bias_ref, w_ref, q_ref, kv_ref, h_ref):
    part = pl.program_id(0)

    @pl.when(part == 0)
    def _():
        gain, bias = gain_ref[...].reshape(1, D), bias_ref[...].reshape(1, D)
        h_ref[...] = layer_norm(x_ref[...].astype(jnp.float32), gain, bias).astype(jnp.bfloat16)

    @pl.when(part == 2)
    def _():
        q_ref[...] = lax.dot_general(h_ref[...], w_ref[0], NT, preferred_element_type=jnp.float32).astype(jnp.bfloat16)

    @pl.when(part < 2)
    def _():
        kv_ref[0] = lax.dot_general(w_ref[0], h_ref[...], NT, preferred_element_type=jnp.float32).astype(jnp.bfloat16)


def encoder_projections(x, gain, bias, w):
    slots, width = x.shape[0], w.shape[1]
    return pl.pallas_call(
        project_kernel,
        grid=(3,),
        in_specs=[
            pl.BlockSpec((slots, D), lambda i: (0, 0)),
            pl.BlockSpec((D,), lambda i: (0,)),
            pl.BlockSpec((D,), lambda i: (0,)),
            pl.BlockSpec((1, width, D), lambda i: ((i + 1) % 3, 0, 0)),
        ],
        out_specs=[
            pl.BlockSpec((slots, width), lambda i: (0, 0)),
            pl.BlockSpec((1, width, slots), lambda i: (jnp.minimum(i, 1), 0, 0)),
        ],
        out_shape=[
            jax.ShapeDtypeStruct((slots, width), jnp.bfloat16),
            jax.ShapeDtypeStruct((2, width, slots), jnp.bfloat16),
        ],
        scratch_shapes=[pltpu.VMEM((slots, D), jnp.bfloat16)],
        cost_estimate=pl.CostEstimate(flops=12 * 10**8, bytes_accessed=5 * 10**6, transcendentals=0),
        name="encoder_projections",
    )(x, gain, bias, w)


def encoder_kernel(q_ref, kv_ref, offset_ref, turn_ref, out_ref, context_ref):
    width = q_ref.shape[1]
    head_size = D // HEADS
    scale = LOG2E / math.sqrt(head_size)
    sums = []
    for low, high, heads in ((0, 256, (0, 1)), (128, width, (2, 3))):
        lanes = lax.broadcasted_iota(jnp.int32, (1, high - low), 1) + low
        window = q_ref[:, low:high]
        result = None
        for head in heads:
            mine = (lanes >= head * head_size) & (lanes < (head + 1) * head_size)
            q = jnp.where(mine, window, jnp.zeros_like(window))
            s = [jnp.dot(q, kv_ref[g, 0, low:high, :], preferred_element_type=jnp.float32) for g in range(GROUP)]
            s = jnp.concatenate(s, axis=1) * scale + offset_ref[...]
            e = jnp.exp2(s - jnp.max(s, axis=1, keepdims=True))
            total = jnp.sum(lane_tiles(e), axis=1, keepdims=True)
            e = e.astype(jnp.bfloat16)
            context = None
            for g in range(GROUP):
                piece = lax.dot_general(
                    e[:, g * SLOTS : (g + 1) * SLOTS],
                    kv_ref[g, 1, low:high, :],
                    NT,
                    preferred_element_type=jnp.float32,
                )
                context = piece if context is None else context + piece
            context = jnp.where(mine, context / total, 0.0)
            result = context if result is None else result + context
        sums.append(result)
    context_ref[:, :128] = sums[0][:, :128].astype(jnp.bfloat16)
    context_ref[:, 128:256] = (sums[0][:, 128:] + sums[1][:, :128]).astype(jnp.bfloat16)
    context_ref[:, 256:] = sums[1][:, 128:].astype(jnp.bfloat16)
    turned = jnp.dot(turn_ref[...], context_ref[...], preferred_element_type=jnp.float32)
    out_ref[...] = turned.astype(jnp.bfloat16)


def encoder_attention(q, kv, offset, turn):
    return pl.pallas_call(
        encoder_kernel,
        in_specs=[pl.BlockSpec(memory_space=pltpu.VMEM)] * 4,
        out_specs=pl.BlockSpec(memory_space=pltpu.VMEM),
        out_shape=jax.ShapeDtypeStruct(q.shape, jnp.bfloat16),
        scratch_shapes=[pltpu.VMEM(q.shape, jnp.bfloat16)],
        cost_estimate=pl.CostEstimate(flops=9 * 10**9, bytes_accessed=5 * 10**6, transcendentals=5 * 10**6),
        name="encoder_attention",
    )(q, kv, offset, turn)


MESH = pl.DeviceIdType.MESH


def finish_kernel(groups, context_ref, w_ref, tokens_ref, gain_ref, bias_ref, dec_ref, out_ref, got, send, recv):
    seq, head = lax.axis_index("seq"), lax.axis_index("head")
    barrier = pltpu.get_barrier_semaphore()
    for step in range(1, groups):
        peer = lax.rem(head + step, groups)
        pl.semaphore_signal(barrier, inc=1, device_id=(seq, peer), device_id_type=MESH)
    pl.semaphore_wait(barrier, groups - 1)
    copies = []
    for step in range(1, groups):
        peer = lax.rem(head + step, groups)
        copy = pltpu.make_async_remote_copy(
            src_ref=context_ref.at[peer],
            dst_ref=got.at[step - 1],
            send_sem=send.at[step - 1],
            recv_sem=recv.at[step - 1],
            device_id=(seq, peer),
            device_id_type=MESH,
        )
        copy.start()
        copies.append(copy)
    total = jnp.dot(context_ref[head], w_ref[head], preferred_element_type=jnp.float32)
    for step in range(1, groups):
        copies[step - 1].wait()
        source = lax.rem(head + groups - step, groups)
        total = total + jnp.dot(got[step - 1], w_ref[source], preferred_element_type=jnp.float32)
    gain, bias = gain_ref[...].reshape(1, D), bias_ref[...].reshape(1, D)
    rows = layer_norm(tokens_ref[...] + total, gain, bias).astype(jnp.bfloat16)
    out_ref[...] = jnp.dot(rows, dec_ref[...], preferred_element_type=jnp.float32).astype(jnp.bfloat16)


def finish_encoder(context, w, tokens, gain, bias, to_decoder):
    groups, width = w.shape[0], w.shape[1]
    return pl.pallas_call(
        lambda *refs: finish_kernel(groups, *refs),
        in_specs=[pl.BlockSpec(memory_space=pltpu.VMEM)] * 6,
        out_specs=pl.BlockSpec(memory_space=pltpu.VMEM),
        out_shape=jax.ShapeDtypeStruct((QUARTER, DD), jnp.bfloat16),
        scratch_shapes=[
            pltpu.VMEM((groups - 1, QUARTER, width), jnp.bfloat16),
            pltpu.SemaphoreType.DMA((groups - 1,)),
            pltpu.SemaphoreType.DMA((groups - 1,)),
        ],
        compiler_params=pltpu.CompilerParams(collective_id=0, has_side_effects=True),
        cost_estimate=pl.CostEstimate(flops=5 * 10**8, bytes_accessed=6 * 10**6, transcendentals=0),
        name="finish_encoder",
    )(context.reshape(groups, QUARTER, width), w, tokens, gain, bias, to_decoder)


def hand_over_kernel(count, groups, x_ref, out_ref, held, send, recv, spread_send, spread_recv):
    seq, head = lax.axis_index("seq"), lax.axis_index("head")
    barrier = pltpu.get_barrier_semaphore()

    def greet(step, carry):
        peer = lax.rem(seq + step, count)
        pl.semaphore_signal(barrier, inc=1, device_id=(peer, head), device_id_type=MESH)
        return carry

    lax.fori_loop(1, count, greet, 0)
    for step in range(1, groups):
        peer = lax.rem(head + step, groups)
        pl.semaphore_signal(barrier, inc=1, device_id=(seq, peer), device_id_type=MESH)
    pl.semaphore_wait(barrier, count + groups - 2)

    def copy_to(step):
        peer = lax.rem(seq + step, count)
        return pltpu.make_async_remote_copy(
            src_ref=x_ref.at[peer],
            dst_ref=held.at[head, seq],
            send_sem=send.at[step],
            recv_sem=recv.at[step],
            device_id=(peer, head),
            device_id_type=MESH,
        )

    def start(step, carry):
        copy_to(step).start()
        return carry

    def finish(step, carry):
        copy_to(step).wait()
        return carry

    lax.fori_loop(1, count, start, 0)
    own = pltpu.make_async_copy(x_ref.at[seq], held.at[head, seq], send.at[0])
    own.start()
    own.wait()
    lax.fori_loop(1, count, finish, 0)
    copies = []
    for step in range(1, groups):
        peer = lax.rem(head + step, groups)
        copy = pltpu.make_async_remote_copy(
            src_ref=held.at[head],
            dst_ref=held.at[head],
            send_sem=spread_send.at[step - 1],
            recv_sem=spread_recv.at[step - 1],
            device_id=(seq, peer),
            device_id_type=MESH,
        )
        copy.start()
        copies.append(copy)
    for copy in copies:
        copy.wait()
    out_ref[...] = held[...]


def hand_over(x, groups):
    count = x.shape[0]
    shape = (groups, *x.shape)
    return pl.pallas_call(
        lambda *refs: hand_over_kernel(count, groups, *refs),
        in_specs=[pl.BlockSpec(memory_space=pltpu.VMEM)],
        out_specs=pl.BlockSpec(memory_space=pltpu.VMEM),
        out_shape=jax.ShapeDtypeStruct(shape, jnp.bfloat16),
        scratch_shapes=[
            pltpu.VMEM(shape, jnp.bfloat16),
            pltpu.SemaphoreType.DMA((count,)),
            pltpu.SemaphoreType.DMA((count,)),
            pltpu.SemaphoreType.DMA((groups - 1,)),
            pltpu.SemaphoreType.DMA((groups - 1,)),
        ],
        compiler_params=pltpu.CompilerParams(collective_id=1, has_side_effects=True),
        name="hand_over",
    )(x)


def body(
    vis_tokens,
    vis_counts,
    vis_spatial,
    enc_gain,
    enc_bias,
    enc_qkv,
    enc_proj,
    final_gain,
    final_bias,
    to_decoder,
    mask_token,
    dec_gain,
    dec_bias,
    dec_qkv,
):
    seq_count = lax.axis_size("seq")
    seq_index = lax.axis_index("seq")
    quarter = lax.axis_index("head")
    clip_index = seq_index % CLIPS
    member = seq_index // CLIPS
    slot_ids = jnp.arange(SLOTS, dtype=jnp.int32)
    starts = jnp.cumsum(vis_counts, axis=1) - vis_counts
    group_counts = lax.dynamic_index_in_dim(vis_counts, clip_index, 0, keepdims=False)
    before = lax.dynamic_slice(starts, (clip_index, member), (1, 1))[0, 0]

    enc_q, enc_kv = encoder_projections(vis_tokens, enc_gain, enc_bias, jnp.swapaxes(enc_qkv, 1, 2))
    groups = [[clip + CLIPS * g for g in range(GROUP)] for clip in range(CLIPS)]
    group_kv = lax.all_gather(enc_kv, "seq", axis_index_groups=groups)
    live = (slot_ids[None, :] < group_counts[:, None]).reshape(1, GROUP * SLOTS)

    frame_ids = jnp.arange(S, dtype=jnp.int32)
    flags = jnp.any(vis_spatial[:, :, None] == frame_ids[None, None, :], axis=1)
    kept = jnp.where(flags, 0.0, 1.0)
    keep_rows = kept.reshape(CLIPS, CHUNKS, CHUNK).transpose(1, 0, 2)
    lane_clip = jnp.arange(CLIPS * HEAD, dtype=jnp.int32) // HEAD
    clip_lanes = (lane_clip[None, :] == jnp.arange(CLIPS)[:, None]).astype(jnp.float32)
    keep = jnp.dot(kept.T, clip_lanes, precision=lax.Precision.HIGHEST).reshape(CHUNKS, CHUNK, CLIPS * HEAD)
    offset_rows = (1.0 - keep_rows) * floor_score
    offsets = jnp.repeat(offset_rows, OWNVIS, axis=1)
    wkv = jnp.concatenate([dec_qkv[1], dec_qkv[2]], axis=1)
    k_masked, v_masked = make_tables(mask_token, dec_gain, dec_bias, wkv, keep)
    own_proj, _ = lax.optimization_barrier((enc_proj, k_masked))
    all_proj = lax.all_gather(own_proj, "head")

    own_ids = jnp.arange(OWN, dtype=jnp.int32)
    own_frame, own_place = own_ids // BLOCK, own_ids % BLOCK
    scale = 1.0 / math.sqrt(HEAD)
    head_of_lane = jnp.arange(2 * HEAD, dtype=jnp.int32) // HEAD

    def split_heads(q):
        q = (q.astype(jnp.bfloat16) * jnp.bfloat16(scale))[None]
        return jnp.where(jnp.arange(2)[:, None, None] == head_of_lane[None, None, :], q, jnp.bfloat16(0))

    own_spatial = lax.dynamic_slice(vis_spatial, (0, seq_index * VB), (CLIPS, VB))
    fine = jnp.concatenate([seq_index * BLOCK + jnp.arange(BLOCK, dtype=jnp.int32), own_spatial.reshape(-1)])
    a1, a2, b1, b2 = angle_tables(jnp.arange(FRAMES, dtype=jnp.int32) * S, fine)
    own_table = a1[:, None, :] * b1[None, :BLOCK] + a2[:, None, :] * b2[None, :BLOCK]
    own_table = own_table.reshape(OWN, DD) + mask_token[None, :]
    base_in = layer_norm(own_table, dec_gain, dec_bias).astype(jnp.bfloat16)
    q_masked = split_heads(jnp.dot(base_in, dec_qkv[0], preferred_element_type=jnp.float32))
    b1, b2 = b1[BLOCK:].reshape(CLIPS, 1, VB, DD), b2[BLOCK:].reshape(CLIPS, 1, VB, DD)
    vis_table = a1[None, :, None, :] * b1 + a2[None, :, None, :] * b2
    base = base_attention(q_masked, k_masked, v_masked, keep_rows)
    source = (slot_ids - before) % SLOTS
    turn = (source[:, None] == slot_ids[None, :]).astype(jnp.bfloat16)
    turn_part = lax.dynamic_slice_in_dim(turn, quarter * QUARTER, QUARTER, 0)
    tokens_part = jnp.dot(turn_part, vis_tokens, preferred_element_type=jnp.float32)
    group_kv, base, tokens_part, vis_table, turn = lax.optimization_barrier(
        (group_kv, base, tokens_part, vis_table, turn)
    )

    def by_clip(_):
        offset = jnp.broadcast_to(
            offset_rows.transpose(1, 0, 2)[:, :, None, :], (CLIPS, CHUNKS, BASE_ROWS, CHUNK)
        )
        accs, ms, ls = lax.map(lambda x: single_attention(q_masked, k_masked, v_masked, x, BASE_ROWS), offset)
        acc = accs[0]
        for clip in range(1, CLIPS):
            acc = jnp.where(lane_clip[None, None, :] == clip, accs[clip], acc)
        return acc, jnp.swapaxes(ms, 0, 1), jnp.swapaxes(ls, 0, 1)

    def shared(_):
        return base[0], jnp.broadcast_to(base[1][:, None], (2, CLIPS, OWN, CHUNK)), base[2]

    vanishing = jnp.min(jnp.sum(base[2], axis=-1)) < 2.0**-60
    base = lax.cond(vanishing, by_clip, shared, None)

    context = encoder_attention(enc_q, group_kv, jnp.where(live, 0.0, floor_score), turn)
    encoded = finish_encoder(context, all_proj, tokens_part, final_gain, final_bias, to_decoder)

    groups = all_proj.shape[0]
    blocks = jnp.pad(encoded.reshape(seq_count, VB * DD // CHUNK, CHUNK), ((0, 0), (0, 4), (0, 0)))
    arrived = hand_over(blocks, groups)[:, :, : VB * DD // CHUNK]
    a_ids = jnp.arange(groups, dtype=jnp.int32)[:, None, None]
    from_ids = jnp.arange(seq_count, dtype=jnp.int32)
    i_ids = jnp.arange(VB, dtype=jnp.int32)[None, None, :]
    from_start = starts.T.reshape(-1)[None, :, None]
    from_count = vis_counts.T.reshape(-1)[None, :, None]
    row = a_ids * VSP + seq_index * VB + i_ids
    offset_in = (row - from_start) % SLOTS
    token = from_start + offset_in
    frame = token // VSP
    target = (from_ids % CLIPS)[None, :, None] * OWNVIS + frame * VB + i_ids
    target = jnp.where(offset_in < from_count, target, -1).reshape(-1)
    pick = (jnp.arange(CLIPS * OWNVIS, dtype=jnp.int32)[:, None] == target[None, :]).astype(jnp.bfloat16)
    own_encoded = jnp.dot(pick, arrived.reshape(-1, DD), preferred_element_type=jnp.float32)

    vis_in = vis_table.reshape(CLIPS * OWNVIS, DD) + own_encoded
    vis_in = layer_norm(vis_in, dec_gain, dec_bias).astype(jnp.bfloat16)
    vis_q, vis_k, vis_v = [jnp.dot(vis_in, dec_qkv[i], preferred_element_type=jnp.float32) for i in range(3)]
    vis_kv = jnp.concatenate([vis_k, vis_v], axis=1).astype(jnp.bfloat16).reshape(CLIPS, OWNVIS, 4 * HEAD)
    all_kv = lax.all_gather(vis_kv, "seq")
    q_visible = split_heads(vis_q)
    single = single_attention(q_visible, k_masked, v_masked, offsets, CLIPS * OWNVIS)

    token_ids = jnp.arange(OWNVIS, dtype=jnp.int32)
    token_place = jnp.repeat(own_spatial[:, None, :] - seq_index * BLOCK, FRAMES, axis=1).reshape(CLIPS, 1, OWNVIS)
    place = (own_frame[None, :, None] == (token_ids // VB)[None, None, :]) & (own_place[None, :, None] == token_place)
    place = place.astype(jnp.float32)

    out = join_attention(q_masked, q_visible, all_kv, base, single, place)
    return out.reshape(CLIPS, FRAMES, BLOCK, 2 * HEAD)


def solution(mesh):
    in_specs = (
        P("seq", None),
        P(),
        P(),
        P(),
        P(),
        P(None, None, "head"),
        P("head", None),
        P(),
        P(),
        P(),
        P(),
        P(),
        P(),
        P(None, None, "head"),
    )
    out_specs = P(None, None, "seq", "head")
    return jax.shard_map(body, mesh=mesh, in_specs=in_specs, out_specs=out_specs, check_vma=False)
```

```python
import math

import jax
import jax.numpy as jnp
from jax import lax
from jax.experimental import pallas as pl
from jax.experimental.pallas import tpu as pltpu
from jax.sharding import PartitionSpec as P

D = 1408
HEADS = 16
DD = 512
DHEADS = 8
S = 1024
BLOCK = 32
VB = 3
GROUP = 8
L = 16384
VSP = 96
VIS = 1536
FRAMES = L // S
CLIPS = 4
SLOTS = 384
QUARTER = 96
CHUNK = 128
CHUNKS = S // CHUNK
KEYS = CHUNK * FRAMES
OWN = FRAMES * BLOCK
OWNVIS = FRAMES * VB
HEAD = DD // DHEADS
LOG2E = 1.4426950408889634
epsilon = 1e-06
floor_score = -1e30
NT = (((1,), (1,)), ((), ()))


def layer_norm(values, gain_row, bias_row):
    centre = jnp.mean(values, axis=-1, keepdims=True)
    centred = values - centre
    spread = jnp.mean(centred * centred, axis=-1, keepdims=True)
    return centred * lax.rsqrt(spread + epsilon) * gain_row + bias_row


def frequencies():
    column_ids = jnp.arange(DD, dtype=jnp.int32)
    exponent = (2 * (column_ids // 2)).astype(jnp.float32) / DD
    return column_ids % 2 == 0, jnp.exp(exponent * -math.log(10000.0))


def sinusoid(positions):
    even, frequency = frequencies()
    angles = positions.astype(jnp.float32)[:, None] * frequency[None, :]
    return jnp.where(even[None, :], jnp.sin(angles), jnp.cos(angles))


TILES = 8


def table_kernel(a1, a2, b1, b2, token, gain, bias, wkv, keep, k_ref, v_ref):
    lanes = lax.broadcasted_iota(jnp.int32, (1, 2 * HEAD), 1)
    for tile in range(TILES):
        rows = pl.ds(tile * CHUNK, CHUNK)
        x = a1[0, tile : tile + 1, :] * b1[...] + a2[0, tile : tile + 1, :] * b2[...] + token[...]
        h = layer_norm(x, gain[...], bias[...]).astype(jnp.bfloat16)
        kv = jnp.dot(h, wkv[...], preferred_element_type=jnp.float32)
        k_ref[rows, :] = kv[:, : 2 * HEAD].astype(jnp.bfloat16)
        v = kv[:, 2 * HEAD :]
        turned = pltpu.roll(v, HEAD, 1)
        for head in range(2):
            twice = jnp.where((lanes < HEAD) == (head == 0), v, turned)
            v_ref[head, rows, :] = (jnp.concatenate([twice, twice], axis=1) * keep[0]).astype(jnp.bfloat16)


def angle_tables(coarse, fine):
    even, frequency = frequencies()
    angle_a = coarse.astype(jnp.float32)[:, None] * frequency[None, :]
    angle_b = fine.astype(jnp.float32)[:, None] * frequency[None, :]
    sin_a, cos_a = jnp.sin(angle_a), jnp.cos(angle_a)
    a1 = jnp.where(even[None, :], sin_a, cos_a)
    a2 = jnp.where(even[None, :], cos_a, -sin_a)
    return lax.optimization_barrier((a1, a2, jnp.cos(angle_b), jnp.sin(angle_b)))


def make_tables(mask_token, dec_gain, dec_bias, wkv, keep):
    coarse = (jnp.arange(FRAMES) * S)[None, :] + (jnp.arange(CHUNKS) * CHUNK)[:, None]
    a1, a2, b1, b2 = angle_tables(coarse.reshape(-1), jnp.arange(CHUNK))
    a1, a2 = a1.reshape(-1, TILES, DD), a2.reshape(-1, TILES, DD)
    steps = a1.shape[0]
    per_chunk = steps // CHUNKS
    whole = lambda *shape: pl.BlockSpec(shape, lambda i: (0,) * len(shape))
    return pl.pallas_call(
        table_kernel,
        grid=(steps,),
        in_specs=[
            pl.BlockSpec((1, TILES, DD), lambda i: (i, 0, 0)),
            pl.BlockSpec((1, TILES, DD), lambda i: (i, 0, 0)),
            whole(CHUNK, DD),
            whole(CHUNK, DD),
            whole(1, DD),
            whole(1, DD),
            whole(1, DD),
            whole(DD, 4 * HEAD),
            pl.BlockSpec((1, CHUNK, CLIPS * HEAD), lambda i: (i // per_chunk, 0, 0)),
        ],
        out_specs=[
            pl.BlockSpec((TILES * CHUNK, 2 * HEAD), lambda i: (i, 0)),
            pl.BlockSpec((2, TILES * CHUNK, CLIPS * HEAD), lambda i: (0, i, 0)),
        ],
        out_shape=[
            jax.ShapeDtypeStruct((L, 2 * HEAD), jnp.bfloat16),
            jax.ShapeDtypeStruct((2, L, CLIPS * HEAD), jnp.bfloat16),
        ],
        cost_estimate=pl.CostEstimate(flops=20 * 10**9, bytes_accessed=25 * 10**6, transcendentals=0),
        name="masked_tables",
    )(a1, a2, b1, b2, mask_token[None], dec_gain[None], dec_bias[None], wkv, keep)


def lane_tiles(x):
    total = x[:, :CHUNK]
    for tile in range(1, x.shape[1] // CHUNK):
        total = total + x[:, tile * CHUNK : (tile + 1) * CHUNK]
    return total


BASE_ROWS = 128
JOIN_ROWS = 512
SLOW_ROWS = 32


def base_kernel(q_ref, k_ref, v_ref, keep_ref, acc_ref, m_ref, l_ref):
    first = pl.program_id(1) == 0

    @pl.when(first)
    def _():
        acc_ref[...] = jnp.zeros_like(acc_ref)
        l_ref[...] = jnp.zeros_like(l_ref)
        m_ref[...] = jnp.full_like(m_ref, floor_score)

    for start in range(0, OWN, BASE_ROWS):
        rows = pl.ds(start, BASE_ROWS)
        s = lax.dot_general(q_ref[0, rows, :], k_ref[...], NT, preferred_element_type=jnp.float32)
        old = m_ref[0, rows, :]
        new = jnp.maximum(old, jnp.max(s, axis=1, keepdims=True))
        factor = jnp.exp2((old - new) * LOG2E)
        e = jnp.exp2((s - new[:, :1]) * LOG2E)
        total = lane_tiles(e)
        for clip in range(CLIPS):
            l_ref[0, clip, rows, :] = l_ref[0, clip, rows, :] * factor + total * keep_ref[0, clip : clip + 1, :]
        m_ref[0, rows, :] = new
        update = jnp.dot(e.astype(jnp.bfloat16), v_ref[0], preferred_element_type=jnp.float32)
        acc_ref[0, rows, :] = acc_ref[0, rows, :] * jnp.concatenate([factor, factor], axis=1) + update


def base_attention(q, k, v4, keep_rows):
    return pl.pallas_call(
        base_kernel,
        grid=(2, CHUNKS),
        in_specs=[
            pl.BlockSpec((1, OWN, 2 * HEAD), lambda h, j: (h, 0, 0)),
            pl.BlockSpec((KEYS, 2 * HEAD), lambda h, j: (j, 0)),
            pl.BlockSpec((1, KEYS, CLIPS * HEAD), lambda h, j: (h, j, 0)),
            pl.BlockSpec((1, CLIPS, CHUNK), lambda h, j: (j, 0, 0)),
        ],
        out_specs=[
            pl.BlockSpec((1, OWN, CLIPS * HEAD), lambda h, j: (h, 0, 0)),
            pl.BlockSpec((1, OWN, CHUNK), lambda h, j: (h, 0, 0)),
            pl.BlockSpec((1, CLIPS, OWN, CHUNK), lambda h, j: (h, 0, 0, 0)),
        ],
        out_shape=[
            jax.ShapeDtypeStruct((2, OWN, CLIPS * HEAD), jnp.float32),
            jax.ShapeDtypeStruct((2, OWN, CHUNK), jnp.float32),
            jax.ShapeDtypeStruct((2, CLIPS, OWN, CHUNK), jnp.float32),
        ],
        cost_estimate=pl.CostEstimate(flops=25 * 10**9, bytes_accessed=25 * 10**6, transcendentals=17 * 10**6),
        name="masked_queries",
    )(q, k, v4, keep_rows)


def single_kernel(q_ref, k_ref, v_ref, offset_ref, acc_ref, m_ref, l_ref):
    @pl.when(pl.program_id(1) == 0)
    def _():
        acc_ref[...] = jnp.zeros_like(acc_ref)
        l_ref[...] = jnp.zeros_like(l_ref)
        m_ref[...] = jnp.full_like(m_ref, floor_score)

    offset = jnp.concatenate([offset_ref[0]] * FRAMES, axis=1)
    for head in range(2):
        s = lax.dot_general(q_ref[head], k_ref[...], NT, preferred_element_type=jnp.float32) + offset
        old = m_ref[head]
        new = jnp.maximum(old, jnp.max(s, axis=1, keepdims=True))
        factor = jnp.exp2((old - new) * LOG2E)
        e = jnp.exp2((s - new[:, :1]) * LOG2E)
        l_ref[head] = l_ref[head] * factor + lane_tiles(e)
        m_ref[head] = new
        update = jnp.dot(e.astype(jnp.bfloat16), v_ref[head], preferred_element_type=jnp.float32)
        acc_ref[head] = acc_ref[head] * jnp.concatenate([factor, factor], axis=1) + update


def single_attention(q, k, v4, offsets, block):
    rows = q.shape[1]
    blocks = rows // block
    offset_map = (lambda r, j: (j, r, 0)) if offsets.shape[1] == rows else (lambda r, j: (j, 0, 0))
    out_spec = lambda width: pl.BlockSpec((2, block, width), lambda r, j: (0, r, 0))
    return pl.pallas_call(
        single_kernel,
        grid=(blocks, CHUNKS),
        in_specs=[
            pl.BlockSpec((2, block, 2 * HEAD), lambda r, j: (0, r, 0)),
            pl.BlockSpec((KEYS, 2 * HEAD), lambda r, j: (j, 0)),
            pl.BlockSpec((2, KEYS, CLIPS * HEAD), lambda r, j: (0, j, 0)),
            pl.BlockSpec((1, block, CHUNK), offset_map),
        ],
        out_specs=[out_spec(CLIPS * HEAD), out_spec(CHUNK), out_spec(CHUNK)],
        out_shape=[
            jax.ShapeDtypeStruct((2, rows, CLIPS * HEAD), jnp.float32),
            jax.ShapeDtypeStruct((2, rows, CHUNK), jnp.float32),
            jax.ShapeDtypeStruct((2, rows, CHUNK), jnp.float32),
        ],
        cost_estimate=pl.CostEstimate(flops=20 * 10**9, bytes_accessed=25 * 10**6, transcendentals=6 * 10**6),
        name="visible_queries" if blocks == 1 else "masked_queries_by_clip",
    )(q, k, v4, offsets)


def own_columns(acc, clip, head):
    piece = jnp.where(clip >= 2, acc[:, CHUNK:], acc[:, :CHUNK])
    return jnp.where(clip % 2 == head, piece, pltpu.roll(piece, HEAD, 1))


def join(q, k, v, acc, m, l):
    s = lax.dot_general(q, k, NT, preferred_element_type=jnp.float32)
    new = jnp.maximum(m, jnp.max(s, axis=1, keepdims=True))
    e = jnp.exp2((s - new[:, :1]) * LOG2E)
    factor = jnp.exp2((m - new) * LOG2E)
    total = jnp.sum(l * factor + lane_tiles(e), axis=1, keepdims=True)
    update = jnp.dot(e.astype(jnp.bfloat16), v, preferred_element_type=jnp.float32)
    return (acc * factor + update) / total


def join_kernel(qb_ref, qv_ref, kv_ref, accb_ref, mb_ref, lb_ref, accv_ref, mv_ref, lv_ref, place_ref, out_ref):
    clip = pl.program_id(0)
    lanes = lax.broadcasted_iota(jnp.int32, (1, 2 * HEAD), 1)
    k = kv_ref[:, 0, :, : 2 * HEAD].reshape(VIS, 2 * HEAD)
    v = kv_ref[:, 0, :, 2 * HEAD :].reshape(VIS, 2 * HEAD)
    place = place_ref[0]
    seen = jnp.sum(place, axis=1, keepdims=True) > 0.5
    for head in range(2):
        mine = (lanes // HEAD) == head
        vis = join(
            qv_ref[head, 0], k, v, own_columns(accv_ref[head, 0], clip, head), mv_ref[head, 0], lv_ref[head, 0]
        ).astype(jnp.bfloat16)
        for start in range(0, OWN, JOIN_ROWS):
            rows = pl.ds(start, JOIN_ROWS)
            base = join(
                qb_ref[head, rows, :],
                k,
                v,
                own_columns(accb_ref[head, rows, :], clip, head),
                mb_ref[head, 0, rows, :],
                lb_ref[head, 0, rows, :],
            )
            spread = jnp.dot(
                place[start : start + JOIN_ROWS].astype(jnp.bfloat16), vis, preferred_element_type=jnp.float32
            )
            value = jnp.where(seen[start : start + JOIN_ROWS], spread, base).astype(jnp.bfloat16)
            if head == 0:
                out_ref[0, rows, :] = value
            else:
                out_ref[0, rows, :] = jnp.where(mine, value, out_ref[0, rows, :])


def join_attention(qb, qv, kv, base, single, place):
    seq_count = kv.shape[0]
    accb, mb, lb = base
    accv, mv, lv = [x.reshape(2, CLIPS, OWNVIS, -1) for x in single]
    vis_spec = lambda width: pl.BlockSpec((2, 1, OWNVIS, width), lambda c: (0, c, 0, 0))
    return pl.pallas_call(
        join_kernel,
        grid=(CLIPS,),
        in_specs=[
            pl.BlockSpec((2, OWN, 2 * HEAD), lambda c: (0, 0, 0)),
            vis_spec(2 * HEAD),
            pl.BlockSpec((seq_count, 1, OWNVIS, 4 * HEAD), lambda c: (0, c, 0, 0)),
            pl.BlockSpec((2, OWN, CLIPS * HEAD), lambda c: (0, 0, 0)),
            pl.BlockSpec((2, 1, OWN, CHUNK), lambda c: (0, c, 0, 0)),
            pl.BlockSpec((2, 1, OWN, CHUNK), lambda c: (0, c, 0, 0)),
            vis_spec(CLIPS * HEAD),
            vis_spec(CHUNK),
            vis_spec(CHUNK),
            pl.BlockSpec((1, OWN, OWNVIS), lambda c: (c, 0, 0)),
        ],
        out_specs=pl.BlockSpec((1, OWN, 2 * HEAD), lambda c: (c, 0, 0)),
        out_shape=jax.ShapeDtypeStruct((CLIPS, OWN, 2 * HEAD), jnp.bfloat16),
        cost_estimate=pl.CostEstimate(flops=8 * 10**9, bytes_accessed=10**7, transcendentals=7 * 10**6),
        name="join_visible_keys",
    )(qb, qv.reshape(2, CLIPS, OWNVIS, -1), kv, accb, mb, lb, accv, mv, lv, place)


def project_kernel(x_ref, gain_ref, bias_ref, w_ref, q_ref, kv_ref, h_ref):
    part = pl.program_id(0)

    @pl.when(part == 0)
    def _():
        gain, bias = gain_ref[...].reshape(1, D), bias_ref[...].reshape(1, D)
        h_ref[...] = layer_norm(x_ref[...].astype(jnp.float32), gain, bias).astype(jnp.bfloat16)

    @pl.when(part == 2)
    def _():
        q_ref[...] = lax.dot_general(h_ref[...], w_ref[0], NT, preferred_element_type=jnp.float32).astype(jnp.bfloat16)

    @pl.when(part < 2)
    def _():
        kv_ref[0] = lax.dot_general(w_ref[0], h_ref[...], NT, preferred_element_type=jnp.float32).astype(jnp.bfloat16)


def encoder_projections(x, gain, bias, w):
    slots, width = x.shape[0], w.shape[1]
    return pl.pallas_call(
        project_kernel,
        grid=(3,),
        in_specs=[
            pl.BlockSpec((slots, D), lambda i: (0, 0)),
            pl.BlockSpec((D,), lambda i: (0,)),
            pl.BlockSpec((D,), lambda i: (0,)),
            pl.BlockSpec((1, width, D), lambda i: ((i + 1) % 3, 0, 0)),
        ],
        out_specs=[
            pl.BlockSpec((slots, width), lambda i: (0, 0)),
            pl.BlockSpec((1, width, slots), lambda i: (jnp.minimum(i, 1), 0, 0)),
        ],
        out_shape=[
            jax.ShapeDtypeStruct((slots, width), jnp.bfloat16),
            jax.ShapeDtypeStruct((2, width, slots), jnp.bfloat16),
        ],
        scratch_shapes=[pltpu.VMEM((slots, D), jnp.bfloat16)],
        cost_estimate=pl.CostEstimate(flops=12 * 10**8, bytes_accessed=5 * 10**6, transcendentals=0),
        name="encoder_projections",
    )(x, gain, bias, w)


def encoder_kernel(q_ref, kv_ref, offset_ref, turn_ref, proj_ref, out_ref, context_ref):
    width = q_ref.shape[1]
    head_size = D // HEADS
    scale = LOG2E / math.sqrt(head_size)
    sums = []
    for low, high, heads in ((0, 256, (0, 1)), (128, width, (2, 3))):
        lanes = lax.broadcasted_iota(jnp.int32, (1, high - low), 1) + low
        window = q_ref[:, low:high]
        result = None
        for head in heads:
            mine = (lanes >= head * head_size) & (lanes < (head + 1) * head_size)
            q = jnp.where(mine, window, jnp.zeros_like(window))
            s = [jnp.dot(q, kv_ref[g, 0, low:high, :], preferred_element_type=jnp.float32) for g in range(GROUP)]
            s = jnp.concatenate(s, axis=1) * scale + offset_ref[...]
            e = jnp.exp2(s - jnp.max(s, axis=1, keepdims=True))
            total = jnp.sum(lane_tiles(e), axis=1, keepdims=True)
            e = e.astype(jnp.bfloat16)
            context = None
            for g in range(GROUP):
                piece = lax.dot_general(
                    e[:, g * SLOTS : (g + 1) * SLOTS],
                    kv_ref[g, 1, low:high, :],
                    NT,
                    preferred_element_type=jnp.float32,
                )
                context = piece if context is None else context + piece
            context = jnp.where(mine, context / total, 0.0)
            result = context if result is None else result + context
        sums.append(result)
    context_ref[:, :128] = sums[0][:, :128].astype(jnp.bfloat16)
    context_ref[:, 128:256] = (sums[0][:, 128:] + sums[1][:, :128]).astype(jnp.bfloat16)
    context_ref[:, 256:] = sums[1][:, 128:].astype(jnp.bfloat16)
    turned = jnp.dot(turn_ref[...], context_ref[...], preferred_element_type=jnp.float32)
    turned = turned.astype(jnp.bfloat16)
    out_ref[...] = jnp.dot(turned, proj_ref[...], preferred_element_type=jnp.float32).astype(jnp.bfloat16)


def encoder_attention(q, kv, offset, turn, proj):
    return pl.pallas_call(
        encoder_kernel,
        in_specs=[pl.BlockSpec(memory_space=pltpu.VMEM)] * 5,
        out_specs=pl.BlockSpec(memory_space=pltpu.VMEM),
        out_shape=jax.ShapeDtypeStruct((q.shape[0], D), jnp.bfloat16),
        scratch_shapes=[pltpu.VMEM(q.shape, jnp.bfloat16)],
        cost_estimate=pl.CostEstimate(flops=9 * 10**9, bytes_accessed=5 * 10**6, transcendentals=5 * 10**6),
        name="encoder_attention",
    )(q, kv, offset, turn, proj)


MESH = pl.DeviceIdType.MESH


def finish_kernel(groups, parts_ref, tokens_ref, gain_ref, bias_ref, dec_ref, out_ref, got, send, recv):
    seq, head = lax.axis_index("seq"), lax.axis_index("head")
    barrier = pltpu.get_barrier_semaphore()
    for step in range(1, groups):
        peer = lax.rem(head + step, groups)
        pl.semaphore_signal(barrier, inc=1, device_id=(seq, peer), device_id_type=MESH)
    pl.semaphore_wait(barrier, groups - 1)
    copies = []
    for step in range(1, groups):
        peer = lax.rem(head + step, groups)
        copy = pltpu.make_async_remote_copy(
            src_ref=parts_ref.at[peer],
            dst_ref=got.at[step - 1],
            send_sem=send.at[step - 1],
            recv_sem=recv.at[step - 1],
            device_id=(seq, peer),
            device_id_type=MESH,
        )
        copy.start()
        copies.append(copy)
    total = tokens_ref[...] + parts_ref[head].astype(jnp.float32)
    for step in range(1, groups):
        copies[step - 1].wait()
        total = total + got[step - 1].astype(jnp.float32)
    gain, bias = gain_ref[...].reshape(1, D), bias_ref[...].reshape(1, D)
    rows = layer_norm(total, gain, bias).astype(jnp.bfloat16)
    out_ref[...] = jnp.dot(rows, dec_ref[...], preferred_element_type=jnp.float32).astype(jnp.bfloat16)


def finish_encoder(parts, tokens, gain, bias, to_decoder):
    groups = parts.shape[0] // QUARTER
    return pl.pallas_call(
        lambda *refs: finish_kernel(groups, *refs),
        in_specs=[pl.BlockSpec(memory_space=pltpu.VMEM)] * 5,
        out_specs=pl.BlockSpec(memory_space=pltpu.VMEM),
        out_shape=jax.ShapeDtypeStruct((QUARTER, DD), jnp.bfloat16),
        scratch_shapes=[
            pltpu.VMEM((groups - 1, QUARTER, D), jnp.bfloat16),
            pltpu.SemaphoreType.DMA((groups - 1,)),
            pltpu.SemaphoreType.DMA((groups - 1,)),
        ],
        compiler_params=pltpu.CompilerParams(collective_id=0, has_side_effects=True),
        cost_estimate=pl.CostEstimate(flops=2 * 10**8, bytes_accessed=3 * 10**6, transcendentals=0),
        name="finish_encoder",
    )(parts.reshape(groups, QUARTER, D), tokens, gain, bias, to_decoder)


def hand_over_kernel(count, groups, x_ref, out_ref, held, send, recv, spread_send, spread_recv):
    seq, head = lax.axis_index("seq"), lax.axis_index("head")
    barrier = pltpu.get_barrier_semaphore()

    def greet(step, carry):
        peer = lax.rem(seq + step, count)
        pl.semaphore_signal(barrier, inc=1, device_id=(peer, head), device_id_type=MESH)
        return carry

    lax.fori_loop(1, count, greet, 0)
    for step in range(1, groups):
        peer = lax.rem(head + step, groups)
        pl.semaphore_signal(barrier, inc=1, device_id=(seq, peer), device_id_type=MESH)
    pl.semaphore_wait(barrier, count + groups - 2)

    def copy_to(step):
        peer = lax.rem(seq + step, count)
        return pltpu.make_async_remote_copy(
            src_ref=x_ref.at[peer],
            dst_ref=held.at[head, seq],
            send_sem=send.at[step],
            recv_sem=recv.at[step],
            device_id=(peer, head),
            device_id_type=MESH,
        )

    def start(step, carry):
        copy_to(step).start()
        return carry

    def finish(step, carry):
        copy_to(step).wait()
        return carry

    lax.fori_loop(1, count, start, 0)
    own = pltpu.make_async_copy(x_ref.at[seq], held.at[head, seq], send.at[0])
    own.start()
    own.wait()
    lax.fori_loop(1, count, finish, 0)
    copies = []
    for step in range(1, groups):
        peer = lax.rem(head + step, groups)
        copy = pltpu.make_async_remote_copy(
            src_ref=held.at[head],
            dst_ref=held.at[head],
            send_sem=spread_send.at[step - 1],
            recv_sem=spread_recv.at[step - 1],
            device_id=(seq, peer),
            device_id_type=MESH,
        )
        copy.start()
        copies.append(copy)
    for copy in copies:
        copy.wait()
    out_ref[...] = held[...]


def hand_over(x, groups):
    count = x.shape[0]
    shape = (groups, *x.shape)
    return pl.pallas_call(
        lambda *refs: hand_over_kernel(count, groups, *refs),
        in_specs=[pl.BlockSpec(memory_space=pltpu.VMEM)],
        out_specs=pl.BlockSpec(memory_space=pltpu.VMEM),
        out_shape=jax.ShapeDtypeStruct(shape, jnp.bfloat16),
        scratch_shapes=[
            pltpu.VMEM(shape, jnp.bfloat16),
            pltpu.SemaphoreType.DMA((count,)),
            pltpu.SemaphoreType.DMA((count,)),
            pltpu.SemaphoreType.DMA((groups - 1,)),
            pltpu.SemaphoreType.DMA((groups - 1,)),
        ],
        compiler_params=pltpu.CompilerParams(collective_id=1, has_side_effects=True),
        name="hand_over",
    )(x)


def body(
    vis_tokens,
    vis_counts,
    vis_spatial,
    enc_gain,
    enc_bias,
    enc_qkv,
    enc_proj,
    final_gain,
    final_bias,
    to_decoder,
    mask_token,
    dec_gain,
    dec_bias,
    dec_qkv,
):
    seq_count = lax.axis_size("seq")
    seq_index = lax.axis_index("seq")
    quarter = lax.axis_index("head")
    clip_index = seq_index % CLIPS
    member = seq_index // CLIPS
    slot_ids = jnp.arange(SLOTS, dtype=jnp.int32)
    starts = jnp.cumsum(vis_counts, axis=1) - vis_counts
    group_counts = lax.dynamic_index_in_dim(vis_counts, clip_index, 0, keepdims=False)
    before = lax.dynamic_slice(starts, (clip_index, member), (1, 1))[0, 0]

    enc_q, enc_kv = encoder_projections(vis_tokens, enc_gain, enc_bias, jnp.swapaxes(enc_qkv, 1, 2))
    groups = [[clip + CLIPS * g for g in range(GROUP)] for clip in range(CLIPS)]
    group_kv = lax.all_gather(enc_kv, "seq", axis_index_groups=groups)
    live = (slot_ids[None, :] < group_counts[:, None]).reshape(1, GROUP * SLOTS)

    frame_ids = jnp.arange(S, dtype=jnp.int32)
    flags = jnp.any(vis_spatial[:, :, None] == frame_ids[None, None, :], axis=1)
    kept = jnp.where(flags, 0.0, 1.0)
    keep_rows = kept.reshape(CLIPS, CHUNKS, CHUNK).transpose(1, 0, 2)
    lane_clip = jnp.arange(CLIPS * HEAD, dtype=jnp.int32) // HEAD
    clip_lanes = (lane_clip[None, :] == jnp.arange(CLIPS)[:, None]).astype(jnp.float32)
    keep = jnp.dot(kept.T, clip_lanes, precision=lax.Precision.HIGHEST).reshape(CHUNKS, CHUNK, CLIPS * HEAD)
    offset_rows = (1.0 - keep_rows) * floor_score
    offsets = jnp.repeat(offset_rows, OWNVIS, axis=1)
    wkv = jnp.concatenate([dec_qkv[1], dec_qkv[2]], axis=1)
    k_masked, v_masked = make_tables(mask_token, dec_gain, dec_bias, wkv, keep)

    own_ids = jnp.arange(OWN, dtype=jnp.int32)
    own_frame, own_place = own_ids // BLOCK, own_ids % BLOCK
    scale = 1.0 / math.sqrt(HEAD)
    head_of_lane = jnp.arange(2 * HEAD, dtype=jnp.int32) // HEAD

    def split_heads(q):
        q = (q.astype(jnp.bfloat16) * jnp.bfloat16(scale))[None]
        return jnp.where(jnp.arange(2)[:, None, None] == head_of_lane[None, None, :], q, jnp.bfloat16(0))

    own_spatial = lax.dynamic_slice(vis_spatial, (0, seq_index * VB), (CLIPS, VB))
    fine = jnp.concatenate([seq_index * BLOCK + jnp.arange(BLOCK, dtype=jnp.int32), own_spatial.reshape(-1)])
    a1, a2, b1, b2 = angle_tables(jnp.arange(FRAMES, dtype=jnp.int32) * S, fine)
    own_table = a1[:, None, :] * b1[None, :BLOCK] + a2[:, None, :] * b2[None, :BLOCK]
    own_table = own_table.reshape(OWN, DD) + mask_token[None, :]
    base_in = layer_norm(own_table, dec_gain, dec_bias).astype(jnp.bfloat16)
    q_masked = split_heads(jnp.dot(base_in, dec_qkv[0], preferred_element_type=jnp.float32))
    b1, b2 = b1[BLOCK:].reshape(CLIPS, 1, VB, DD), b2[BLOCK:].reshape(CLIPS, 1, VB, DD)
    vis_table = a1[None, :, None, :] * b1 + a2[None, :, None, :] * b2
    base = base_attention(q_masked, k_masked, v_masked, keep_rows)
    source = (slot_ids - before) % SLOTS
    turn = (source[:, None] == slot_ids[None, :]).astype(jnp.bfloat16)
    turn_part = lax.dynamic_slice_in_dim(turn, quarter * QUARTER, QUARTER, 0)
    tokens_part = jnp.dot(turn_part, vis_tokens, preferred_element_type=jnp.float32)
    group_kv, base, tokens_part, vis_table, turn = lax.optimization_barrier(
        (group_kv, base, tokens_part, vis_table, turn)
    )

    def by_clip(_):
        offset = jnp.broadcast_to(
            offset_rows.transpose(1, 0, 2)[:, :, None, :], (CLIPS, CHUNKS, SLOW_ROWS, CHUNK)
        )
        accs, ms, ls = lax.map(lambda x: single_attention(q_masked, k_masked, v_masked, x, SLOW_ROWS), offset)
        acc = accs[0]
        for clip in range(1, CLIPS):
            acc = jnp.where(lane_clip[None, None, :] == clip, accs[clip], acc)
        return acc, jnp.swapaxes(ms, 0, 1), jnp.swapaxes(ls, 0, 1)

    def shared(_):
        return base[0], jnp.broadcast_to(base[1][:, None], (2, CLIPS, OWN, CHUNK)), base[2]

    vanishing = jnp.min(jnp.sum(base[2], axis=-1)) < 2.0**-60
    base = lax.cond(vanishing, by_clip, shared, None)

    parts = encoder_attention(enc_q, group_kv, jnp.where(live, 0.0, floor_score), turn, enc_proj)
    encoded = finish_encoder(parts, tokens_part, final_gain, final_bias, to_decoder)

    groups = lax.axis_size("head")
    blocks = jnp.pad(encoded.reshape(seq_count, VB * DD // CHUNK, CHUNK), ((0, 0), (0, 4), (0, 0)))
    arrived = hand_over(blocks, groups)[:, :, : VB * DD // CHUNK]
    a_ids = jnp.arange(groups, dtype=jnp.int32)[:, None, None]
    from_ids = jnp.arange(seq_count, dtype=jnp.int32)
    i_ids = jnp.arange(VB, dtype=jnp.int32)[None, None, :]
    from_start = starts.T.reshape(-1)[None, :, None]
    from_count = vis_counts.T.reshape(-1)[None, :, None]
    row = a_ids * VSP + seq_index * VB + i_ids
    offset_in = (row - from_start) % SLOTS
    token = from_start + offset_in
    frame = token // VSP
    target = (from_ids % CLIPS)[None, :, None] * OWNVIS + frame * VB + i_ids
    target = jnp.where(offset_in < from_count, target, -1).reshape(-1)
    pick = (jnp.arange(CLIPS * OWNVIS, dtype=jnp.int32)[:, None] == target[None, :]).astype(jnp.bfloat16)
    own_encoded = jnp.dot(pick, arrived.reshape(-1, DD), preferred_element_type=jnp.float32)

    vis_in = vis_table.reshape(CLIPS * OWNVIS, DD) + own_encoded
    vis_in = layer_norm(vis_in, dec_gain, dec_bias).astype(jnp.bfloat16)
    vis_q, vis_k, vis_v = [jnp.dot(vis_in, dec_qkv[i], preferred_element_type=jnp.float32) for i in range(3)]
    vis_kv = jnp.concatenate([vis_k, vis_v], axis=1).astype(jnp.bfloat16).reshape(CLIPS, OWNVIS, 4 * HEAD)
    all_kv = lax.all_gather(vis_kv, "seq")
    q_visible = split_heads(vis_q)
    single = single_attention(q_visible, k_masked, v_masked, offsets, CLIPS * OWNVIS)

    token_ids = jnp.arange(OWNVIS, dtype=jnp.int32)
    token_place = jnp.repeat(own_spatial[:, None, :] - seq_index * BLOCK, FRAMES, axis=1).reshape(CLIPS, 1, OWNVIS)
    place = (own_frame[None, :, None] == (token_ids // VB)[None, None, :]) & (own_place[None, :, None] == token_place)
    place = place.astype(jnp.float32)

    out = join_attention(q_masked, q_visible, all_kv, base, single, place)
    return out.reshape(CLIPS, FRAMES, BLOCK, 2 * HEAD)


def solution(mesh):
    in_specs = (
        P("seq", None),
        P(),
        P(),
        P(),
        P(),
        P(None, None, "head"),
        P("head", None),
        P(),
        P(),
        P(),
        P(),
        P(),
        P(),
        P(None, None, "head"),
    )
    out_specs = P(None, None, "seq", "head")
    return jax.shard_map(body, mesh=mesh, in_specs=in_specs, out_specs=out_specs, check_vma=False)
```

```python
import math

import jax
import jax.numpy as jnp
from jax import lax
from jax.experimental import pallas as pl
from jax.experimental.pallas import tpu as pltpu
from jax.sharding import PartitionSpec as P

D = 1408
HEADS = 16
DD = 512
DHEADS = 8
S = 1024
BLOCK = 32
VB = 3
GROUP = 8
L = 16384
VSP = 96
VIS = 1536
FRAMES = L // S
CLIPS = 4
SLOTS = 384
QUARTER = 96
CHUNK = 128
CHUNKS = S // CHUNK
KEYS = CHUNK * FRAMES
OWN = FRAMES * BLOCK
OWNVIS = FRAMES * VB
HEAD = DD // DHEADS
LOG2E = 1.4426950408889634
epsilon = 1e-06
floor_score = -1e30
NT = (((1,), (1,)), ((), ()))


def layer_norm(values, gain_row, bias_row):
    centre = jnp.mean(values, axis=-1, keepdims=True)
    centred = values - centre
    spread = jnp.mean(centred * centred, axis=-1, keepdims=True)
    return centred * lax.rsqrt(spread + epsilon) * gain_row + bias_row


def frequencies():
    column_ids = jnp.arange(DD, dtype=jnp.int32)
    exponent = (2 * (column_ids // 2)).astype(jnp.float32) / DD
    return column_ids % 2 == 0, jnp.exp(exponent * -math.log(10000.0))


def sinusoid(positions):
    even, frequency = frequencies()
    angles = positions.astype(jnp.float32)[:, None] * frequency[None, :]
    return jnp.where(even[None, :], jnp.sin(angles), jnp.cos(angles))


TILES = 4


def table_tile(tile, a1, a2, b1, b2, token, gain, bias, wkv, keep, k_ref, v_ref):
    lanes = lax.broadcasted_iota(jnp.int32, (1, 2 * HEAD), 1)
    rows = pl.ds(pl.multiple_of(tile * CHUNK, CHUNK), CHUNK)
    one = pl.ds(tile, 1)
    x = a1[0, one, :] * b1[...] + a2[0, one, :] * b2[...] + token[...]
    h = layer_norm(x, gain[...], bias[...]).astype(jnp.bfloat16)
    kv = jnp.dot(h, wkv[...], preferred_element_type=jnp.float32)
    k_ref[rows, :] = kv[:, : 2 * HEAD].astype(jnp.bfloat16)
    v = kv[:, 2 * HEAD :]
    turned = pltpu.roll(v, HEAD, 1)
    for head in range(2):
        twice = jnp.where((lanes < HEAD) == (head == 0), v, turned)
        v_ref[head, rows, :] = (jnp.concatenate([twice, twice], axis=1) * keep[0]).astype(jnp.bfloat16)


MESH = pl.DeviceIdType.MESH


def masked_kernel(
    a1, a2, b1, b2, token, gain, bias, wkv, keep, q_ref, keep_rows, kv_ref, k_ref, v_ref, acc_ref, m_ref, l_ref,
    others_ref, send, recv,
):
    step = pl.program_id(0)
    seq, head = lax.axis_index("seq"), lax.axis_index("head")
    member, clip = seq // CLIPS, lax.rem(seq, CLIPS)

    def peer(distance):
        return (lax.rem(member + distance, GROUP) * CLIPS + clip, head)

    def copy_to(distance):
        return pltpu.make_async_remote_copy(
            src_ref=kv_ref,
            dst_ref=others_ref.at[distance - 1],
            send_sem=send.at[distance - 1],
            recv_sem=recv.at[distance - 1],
            device_id=peer(distance),
            device_id_type=MESH,
        )

    @pl.when(step == 0)
    def _():
        barrier = pltpu.get_barrier_semaphore()
        for distance in range(1, GROUP):
            pl.semaphore_signal(barrier, inc=1, device_id=peer(distance), device_id_type=MESH)
        pl.semaphore_wait(barrier, GROUP - 1)
        for distance in range(1, GROUP):
            copy_to(distance).start()
        acc_ref[...] = jnp.zeros_like(acc_ref)
        l_ref[...] = jnp.zeros_like(l_ref)
        m_ref[...] = jnp.full_like(m_ref, floor_score)

    def tiles(part, carry):
        for tile in range(TILES):
            table_tile(part * TILES + tile, a1, a2, b1, b2, token, gain, bias, wkv, keep, k_ref, v_ref)
        return carry

    lax.fori_loop(0, FRAMES // TILES, tiles, 0)
    base_chunk(q_ref, k_ref, v_ref, keep_rows, acc_ref, m_ref, l_ref)

    @pl.when(step == CHUNKS - 1)
    def _():
        for distance in range(1, GROUP):
            copy_to(distance).wait()


def angle_tables(coarse, fine):
    even, frequency = frequencies()
    angle_a = coarse.astype(jnp.float32)[:, None] * frequency[None, :]
    angle_b = fine.astype(jnp.float32)[:, None] * frequency[None, :]
    sin_a, cos_a = jnp.sin(angle_a), jnp.cos(angle_a)
    a1 = jnp.where(even[None, :], sin_a, cos_a)
    a2 = jnp.where(even[None, :], cos_a, -sin_a)
    return lax.optimization_barrier((a1, a2, jnp.cos(angle_b), jnp.sin(angle_b)))


def masked_part(mask_token, dec_gain, dec_bias, wkv, keep, q, keep_rows, kv):
    coarse = (jnp.arange(FRAMES) * S)[None, :] + (jnp.arange(CHUNKS) * CHUNK)[:, None]
    a1, a2, b1, b2 = angle_tables(coarse.reshape(-1), jnp.arange(CHUNK))
    a1, a2 = a1.reshape(CHUNKS, FRAMES, DD), a2.reshape(CHUNKS, FRAMES, DD)
    whole = lambda *shape: pl.BlockSpec(shape, lambda i: (0,) * len(shape))
    return pl.pallas_call(
        masked_kernel,
        grid=(CHUNKS,),
        in_specs=[
            pl.BlockSpec((1, FRAMES, DD), lambda i: (i, 0, 0)),
            pl.BlockSpec((1, FRAMES, DD), lambda i: (i, 0, 0)),
            whole(CHUNK, DD),
            whole(CHUNK, DD),
            whole(1, DD),
            whole(1, DD),
            whole(1, DD),
            whole(DD, 4 * HEAD),
            pl.BlockSpec((1, CHUNK, CLIPS * HEAD), lambda i: (i, 0, 0)),
            whole(1, OWN, 2 * HEAD),
            pl.BlockSpec((1, CLIPS, CHUNK), lambda i: (i, 0, 0)),
            pl.BlockSpec(memory_space=pl.ANY),
        ],
        out_specs=[
            pl.BlockSpec((KEYS, 2 * HEAD), lambda i: (i, 0)),
            pl.BlockSpec((2, KEYS, CLIPS * HEAD), lambda i: (0, i, 0)),
            whole(1, OWN, CLIPS * HEAD),
            whole(1, OWN, CHUNK),
            whole(1, CLIPS, OWN, CHUNK),
            pl.BlockSpec(memory_space=pl.ANY),
        ],
        out_shape=[
            jax.ShapeDtypeStruct((L, 2 * HEAD), jnp.bfloat16),
            jax.ShapeDtypeStruct((2, L, CLIPS * HEAD), jnp.bfloat16),
            jax.ShapeDtypeStruct((1, OWN, CLIPS * HEAD), jnp.float32),
            jax.ShapeDtypeStruct((1, OWN, CHUNK), jnp.float32),
            jax.ShapeDtypeStruct((1, CLIPS, OWN, CHUNK), jnp.float32),
            jax.ShapeDtypeStruct((GROUP - 1, *kv.shape), jnp.bfloat16),
        ],
        scratch_shapes=[pltpu.SemaphoreType.DMA((GROUP - 1,)), pltpu.SemaphoreType.DMA((GROUP - 1,))],
        compiler_params=pltpu.CompilerParams(collective_id=2, has_side_effects=True),
        cost_estimate=pl.CostEstimate(flops=40 * 10**9, bytes_accessed=35 * 10**6, transcendentals=9 * 10**6),
        name="masked_part",
    )(a1, a2, b1, b2, mask_token[None], dec_gain[None], dec_bias[None], wkv, keep, q, keep_rows, kv)


def lane_tiles(x):
    total = x[:, :CHUNK]
    for tile in range(1, x.shape[1] // CHUNK):
        total = total + x[:, tile * CHUNK : (tile + 1) * CHUNK]
    return total


BASE_ROWS = 128
SLOW_ROWS = 16


def base_kernel(q_ref, k_ref, v_ref, keep_ref, acc_ref, m_ref, l_ref):
    @pl.when(pl.program_id(0) == 0)
    def _():
        acc_ref[...] = jnp.zeros_like(acc_ref)
        l_ref[...] = jnp.zeros_like(l_ref)
        m_ref[...] = jnp.full_like(m_ref, floor_score)

    base_chunk(q_ref, k_ref, v_ref, keep_ref, acc_ref, m_ref, l_ref)


def base_chunk(q_ref, k_ref, v_ref, keep_ref, acc_ref, m_ref, l_ref):
    for start in range(0, OWN, BASE_ROWS):
        rows = pl.ds(start, BASE_ROWS)
        s = lax.dot_general(q_ref[0, rows, :], k_ref[...], NT, preferred_element_type=jnp.float32)
        old = m_ref[0, rows, :]
        new = jnp.maximum(old, jnp.max(s, axis=1, keepdims=True))
        factor = jnp.exp2((old - new) * LOG2E)
        e = jnp.exp2((s - new[:, :1]) * LOG2E)
        total = lane_tiles(e)
        for clip in range(CLIPS):
            l_ref[0, clip, rows, :] = l_ref[0, clip, rows, :] * factor + total * keep_ref[0, clip : clip + 1, :]
        m_ref[0, rows, :] = new
        update = jnp.dot(e.astype(jnp.bfloat16), v_ref[0], preferred_element_type=jnp.float32)
        acc_ref[0, rows, :] = acc_ref[0, rows, :] * jnp.concatenate([factor, factor], axis=1) + update


def base_attention(head, q, k, v4, keep_rows):
    return pl.pallas_call(
        base_kernel,
        grid=(CHUNKS,),
        in_specs=[
            pl.BlockSpec((1, OWN, 2 * HEAD), lambda j: (0, 0, 0)),
            pl.BlockSpec((KEYS, 2 * HEAD), lambda j: (j, 0)),
            pl.BlockSpec((1, KEYS, CLIPS * HEAD), lambda j: (head, j, 0)),
            pl.BlockSpec((1, CLIPS, CHUNK), lambda j: (j, 0, 0)),
        ],
        out_specs=[
            pl.BlockSpec((1, OWN, CLIPS * HEAD), lambda j: (0, 0, 0)),
            pl.BlockSpec((1, OWN, CHUNK), lambda j: (0, 0, 0)),
            pl.BlockSpec((1, CLIPS, OWN, CHUNK), lambda j: (0, 0, 0, 0)),
        ],
        out_shape=[
            jax.ShapeDtypeStruct((1, OWN, CLIPS * HEAD), jnp.float32),
            jax.ShapeDtypeStruct((1, OWN, CHUNK), jnp.float32),
            jax.ShapeDtypeStruct((1, CLIPS, OWN, CHUNK), jnp.float32),
        ],
        cost_estimate=pl.CostEstimate(flops=20 * 10**9, bytes_accessed=15 * 10**6, transcendentals=9 * 10**6),
        name="masked_queries",
    )(q, k, v4, keep_rows)


def single_kernel(q_ref, k_ref, v_ref, offset_ref, acc_ref, m_ref, l_ref):
    @pl.when(pl.program_id(1) == 0)
    def _():
        acc_ref[...] = jnp.zeros_like(acc_ref)
        l_ref[...] = jnp.zeros_like(l_ref)
        m_ref[...] = jnp.full_like(m_ref, floor_score)

    offset = jnp.concatenate([offset_ref[0]] * FRAMES, axis=1)
    for head in range(2):
        s = lax.dot_general(q_ref[head], k_ref[...], NT, preferred_element_type=jnp.float32) + offset
        old = m_ref[head]
        new = jnp.maximum(old, jnp.max(s, axis=1, keepdims=True))
        factor = jnp.exp2((old - new) * LOG2E)
        e = jnp.exp2((s - new[:, :1]) * LOG2E)
        l_ref[head] = l_ref[head] * factor + lane_tiles(e)
        m_ref[head] = new
        update = jnp.dot(e.astype(jnp.bfloat16), v_ref[head], preferred_element_type=jnp.float32)
        acc_ref[head] = acc_ref[head] * jnp.concatenate([factor, factor], axis=1) + update


def single_attention(q, k, v4, offsets, block):
    rows = q.shape[1]
    blocks = rows // block
    offset_map = (lambda r, j: (j, r, 0)) if offsets.shape[1] == rows else (lambda r, j: (j, 0, 0))
    out_spec = lambda width: pl.BlockSpec((2, block, width), lambda r, j: (0, r, 0))
    return pl.pallas_call(
        single_kernel,
        grid=(blocks, CHUNKS),
        in_specs=[
            pl.BlockSpec((2, block, 2 * HEAD), lambda r, j: (0, r, 0)),
            pl.BlockSpec((KEYS, 2 * HEAD), lambda r, j: (j, 0)),
            pl.BlockSpec((2, KEYS, CLIPS * HEAD), lambda r, j: (0, j, 0)),
            pl.BlockSpec((1, block, CHUNK), offset_map),
        ],
        out_specs=[out_spec(CLIPS * HEAD), out_spec(CHUNK), out_spec(CHUNK)],
        out_shape=[
            jax.ShapeDtypeStruct((2, rows, CLIPS * HEAD), jnp.float32),
            jax.ShapeDtypeStruct((2, rows, CHUNK), jnp.float32),
            jax.ShapeDtypeStruct((2, rows, CHUNK), jnp.float32),
        ],
        cost_estimate=pl.CostEstimate(flops=20 * 10**9, bytes_accessed=25 * 10**6, transcendentals=6 * 10**6),
        name="visible_queries" if blocks == 1 else "masked_queries_by_clip",
    )(q, k, v4, offsets)


def own_columns(acc, clip, head):
    piece = jnp.where(clip >= 2, acc[:, CHUNK:], acc[:, :CHUNK])
    return jnp.where(clip % 2 == head, piece, pltpu.roll(piece, HEAD, 1))


def join(q, k, v, acc, m, l):
    s = lax.dot_general(q, k, NT, preferred_element_type=jnp.float32)
    new = jnp.maximum(m, jnp.max(s, axis=1, keepdims=True))
    e = jnp.exp2((s - new[:, :1]) * LOG2E)
    factor = jnp.exp2((m - new) * LOG2E)
    total = jnp.sum(l * factor + lane_tiles(e), axis=1, keepdims=True)
    update = jnp.dot(e.astype(jnp.bfloat16), v, preferred_element_type=jnp.float32)
    return (acc * factor + update) / total


def join_kernel(qb_ref, qv_ref, kv_ref, accb_ref, mb_ref, lb_ref, accv_ref, mv_ref, lv_ref, place_ref, out_ref):
    clip, head = pl.program_id(0), pl.program_id(1)
    lanes = lax.broadcasted_iota(jnp.int32, (1, 2 * HEAD), 1)
    k = kv_ref[:, 0, :, : 2 * HEAD].reshape(VIS, 2 * HEAD)
    v = kv_ref[:, 0, :, 2 * HEAD :].reshape(VIS, 2 * HEAD)
    place = place_ref[0]
    seen = jnp.sum(place, axis=1, keepdims=True) > 0.5
    vis = join(qv_ref[0, 0], k, v, own_columns(accv_ref[0, 0], clip, head), mv_ref[0, 0], lv_ref[0, 0])
    base = join(qb_ref[0], k, v, own_columns(accb_ref[0], clip, head), mb_ref[0, 0], lb_ref[0, 0])
    spread = jnp.dot(place.astype(jnp.bfloat16), vis.astype(jnp.bfloat16), preferred_element_type=jnp.float32)
    value = jnp.where(seen, spread, base).astype(jnp.bfloat16)

    @pl.when(head == 0)
    def _():
        out_ref[0] = value

    @pl.when(head == 1)
    def _():
        out_ref[0] = jnp.where(lanes >= HEAD, value, out_ref[0])


def join_attention(qb, qv, kv, base, single, place):
    seq_count = kv.shape[0]
    accb, mb, lb = base
    accv, mv, lv = [x.reshape(2, CLIPS, OWNVIS, -1) for x in single]
    vis_spec = lambda width: pl.BlockSpec((1, 1, OWNVIS, width), lambda c, h: (h, c, 0, 0))
    return pl.pallas_call(
        join_kernel,
        grid=(CLIPS, 2),
        in_specs=[
            pl.BlockSpec((1, OWN, 2 * HEAD), lambda c, h: (h, 0, 0)),
            vis_spec(2 * HEAD),
            pl.BlockSpec((seq_count, 1, OWNVIS, 4 * HEAD), lambda c, h: (0, c, 0, 0)),
            pl.BlockSpec((1, OWN, CLIPS * HEAD), lambda c, h: (h, 0, 0)),
            pl.BlockSpec((1, 1, OWN, CHUNK), lambda c, h: (h, c, 0, 0)),
            pl.BlockSpec((1, 1, OWN, CHUNK), lambda c, h: (h, c, 0, 0)),
            vis_spec(CLIPS * HEAD),
            vis_spec(CHUNK),
            vis_spec(CHUNK),
            pl.BlockSpec((1, OWN, OWNVIS), lambda c, h: (c, 0, 0)),
        ],
        out_specs=pl.BlockSpec((1, OWN, 2 * HEAD), lambda c, h: (c, 0, 0)),
        out_shape=jax.ShapeDtypeStruct((CLIPS, OWN, 2 * HEAD), jnp.bfloat16),
        cost_estimate=pl.CostEstimate(flops=8 * 10**9, bytes_accessed=10**7, transcendentals=7 * 10**6),
        name="join_visible_keys",
    )(qb, qv.reshape(2, CLIPS, OWNVIS, -1), kv, accb, mb, lb, accv, mv, lv, place)


def project_kernel(x_ref, gain_ref, bias_ref, w_ref, q_ref, kv_ref, h_ref):
    part = pl.program_id(0)

    @pl.when(part == 0)
    def _():
        gain, bias = gain_ref[...].reshape(1, D), bias_ref[...].reshape(1, D)
        h_ref[...] = layer_norm(x_ref[...].astype(jnp.float32), gain, bias).astype(jnp.bfloat16)

    @pl.when(part == 2)
    def _():
        q_ref[...] = lax.dot_general(h_ref[...], w_ref[0], NT, preferred_element_type=jnp.float32).astype(jnp.bfloat16)

    @pl.when(part < 2)
    def _():
        kv_ref[0] = lax.dot_general(w_ref[0], h_ref[...], NT, preferred_element_type=jnp.float32).astype(jnp.bfloat16)


def encoder_projections(x, gain, bias, w):
    slots, width = x.shape[0], w.shape[1]
    return pl.pallas_call(
        project_kernel,
        grid=(3,),
        in_specs=[
            pl.BlockSpec((slots, D), lambda i: (0, 0)),
            pl.BlockSpec((D,), lambda i: (0,)),
            pl.BlockSpec((D,), lambda i: (0,)),
            pl.BlockSpec((1, width, D), lambda i: ((i + 1) % 3, 0, 0)),
        ],
        out_specs=[
            pl.BlockSpec((slots, width), lambda i: (0, 0)),
            pl.BlockSpec((1, width, slots), lambda i: (jnp.minimum(i, 1), 0, 0)),
        ],
        out_shape=[
            jax.ShapeDtypeStruct((slots, width), jnp.bfloat16),
            jax.ShapeDtypeStruct((2, width, slots), jnp.bfloat16),
        ],
        scratch_shapes=[pltpu.VMEM((slots, D), jnp.bfloat16)],
        cost_estimate=pl.CostEstimate(flops=12 * 10**8, bytes_accessed=5 * 10**6, transcendentals=0),
        name="encoder_projections",
    )(x, gain, bias, w)


def encoder_kernel(q_ref, own_ref, others_ref, offset_ref, turn_ref, proj_ref, out_ref, context_ref):
    width = q_ref.shape[1]
    head_size = D // HEADS
    scale = LOG2E / math.sqrt(head_size)
    members = [own_ref] + [others_ref.at[g] for g in range(GROUP - 1)]
    sums = []
    for low, high, heads in ((0, 256, (0, 1)), (128, width, (2, 3))):
        lanes = lax.broadcasted_iota(jnp.int32, (1, high - low), 1) + low
        window = q_ref[:, low:high]
        result = None
        for head in heads:
            mine = (lanes >= head * head_size) & (lanes < (head + 1) * head_size)
            q = jnp.where(mine, window, jnp.zeros_like(window))
            s = [jnp.dot(q, members[g][0, low:high, :], preferred_element_type=jnp.float32) for g in range(GROUP)]
            s = jnp.concatenate(s, axis=1) * scale + offset_ref[...]
            e = jnp.exp2(s - jnp.max(s, axis=1, keepdims=True))
            total = jnp.sum(lane_tiles(e), axis=1, keepdims=True)
            e = e.astype(jnp.bfloat16)
            context = None
            for g in range(GROUP):
                piece = lax.dot_general(
                    e[:, g * SLOTS : (g + 1) * SLOTS],
                    members[g][1, low:high, :],
                    NT,
                    preferred_element_type=jnp.float32,
                )
                context = piece if context is None else context + piece
            context = jnp.where(mine, context / total, 0.0)
            result = context if result is None else result + context
        sums.append(result)
    context_ref[:, :128] = sums[0][:, :128].astype(jnp.bfloat16)
    context_ref[:, 128:256] = (sums[0][:, 128:] + sums[1][:, :128]).astype(jnp.bfloat16)
    context_ref[:, 256:] = sums[1][:, 128:].astype(jnp.bfloat16)
    turned = jnp.dot(turn_ref[...], context_ref[...], preferred_element_type=jnp.float32)
    turned = turned.astype(jnp.bfloat16)
    out_ref[...] = jnp.dot(turned, proj_ref[...], preferred_element_type=jnp.float32).astype(jnp.bfloat16)


def encoder_attention(q, own, others, offset, turn, proj):
    return pl.pallas_call(
        encoder_kernel,
        in_specs=[pl.BlockSpec(memory_space=pltpu.VMEM)] * 6,
        out_specs=pl.BlockSpec(memory_space=pltpu.VMEM),
        out_shape=jax.ShapeDtypeStruct((q.shape[0], D), jnp.bfloat16),
        scratch_shapes=[pltpu.VMEM(q.shape, jnp.bfloat16)],
        cost_estimate=pl.CostEstimate(flops=9 * 10**9, bytes_accessed=5 * 10**6, transcendentals=5 * 10**6),
        name="encoder_attention",
    )(q, own, others, offset, turn, proj)


def finish_kernel(groups, parts_ref, tokens_ref, gain_ref, bias_ref, dec_ref, out_ref, got, send, recv):
    seq, head = lax.axis_index("seq"), lax.axis_index("head")
    barrier = pltpu.get_barrier_semaphore()
    for step in range(1, groups):
        peer = lax.rem(head + step, groups)
        pl.semaphore_signal(barrier, inc=1, device_id=(seq, peer), device_id_type=MESH)
    pl.semaphore_wait(barrier, groups - 1)
    copies = []
    for step in range(1, groups):
        peer = lax.rem(head + step, groups)
        copy = pltpu.make_async_remote_copy(
            src_ref=parts_ref.at[peer],
            dst_ref=got.at[step - 1],
            send_sem=send.at[step - 1],
            recv_sem=recv.at[step - 1],
            device_id=(seq, peer),
            device_id_type=MESH,
        )
        copy.start()
        copies.append(copy)
    total = tokens_ref[...] + parts_ref[head].astype(jnp.float32)
    for step in range(1, groups):
        copies[step - 1].wait()
        total = total + got[step - 1].astype(jnp.float32)
    gain, bias = gain_ref[...].reshape(1, D), bias_ref[...].reshape(1, D)
    rows = layer_norm(total, gain, bias).astype(jnp.bfloat16)
    out_ref[...] = jnp.dot(rows, dec_ref[...], preferred_element_type=jnp.float32).astype(jnp.bfloat16)


def finish_encoder(parts, tokens, gain, bias, to_decoder):
    groups = parts.shape[0] // QUARTER
    return pl.pallas_call(
        lambda *refs: finish_kernel(groups, *refs),
        in_specs=[pl.BlockSpec(memory_space=pltpu.VMEM)] * 5,
        out_specs=pl.BlockSpec(memory_space=pltpu.VMEM),
        out_shape=jax.ShapeDtypeStruct((QUARTER, DD), jnp.bfloat16),
        scratch_shapes=[
            pltpu.VMEM((groups - 1, QUARTER, D), jnp.bfloat16),
            pltpu.SemaphoreType.DMA((groups - 1,)),
            pltpu.SemaphoreType.DMA((groups - 1,)),
        ],
        compiler_params=pltpu.CompilerParams(collective_id=0, has_side_effects=True),
        cost_estimate=pl.CostEstimate(flops=2 * 10**8, bytes_accessed=3 * 10**6, transcendentals=0),
        name="finish_encoder",
    )(parts.reshape(groups, QUARTER, D), tokens, gain, bias, to_decoder)


def hand_over_kernel(count, groups, x_ref, out_ref, held, send, recv, spread_send, spread_recv):
    seq, head = lax.axis_index("seq"), lax.axis_index("head")
    barrier = pltpu.get_barrier_semaphore()

    def greet(step, carry):
        peer = lax.rem(seq + step, count)
        pl.semaphore_signal(barrier, inc=1, device_id=(peer, head), device_id_type=MESH)
        return carry

    lax.fori_loop(1, count, greet, 0)
    for step in range(1, groups):
        peer = lax.rem(head + step, groups)
        pl.semaphore_signal(barrier, inc=1, device_id=(seq, peer), device_id_type=MESH)
    pl.semaphore_wait(barrier, count + groups - 2)

    def copy_to(step):
        peer = lax.rem(seq + step, count)
        return pltpu.make_async_remote_copy(
            src_ref=x_ref.at[peer],
            dst_ref=held.at[head, seq],
            send_sem=send.at[step],
            recv_sem=recv.at[step],
            device_id=(peer, head),
            device_id_type=MESH,
        )

    def start(step, carry):
        copy_to(step).start()
        return carry

    def finish(step, carry):
        copy_to(step).wait()
        return carry

    lax.fori_loop(1, count, start, 0)
    own = pltpu.make_async_copy(x_ref.at[seq], held.at[head, seq], send.at[0])
    own.start()
    own.wait()
    lax.fori_loop(1, count, finish, 0)
    copies = []
    for step in range(1, groups):
        peer = lax.rem(head + step, groups)
        copy = pltpu.make_async_remote_copy(
            src_ref=held.at[head],
            dst_ref=held.at[head],
            send_sem=spread_send.at[step - 1],
            recv_sem=spread_recv.at[step - 1],
            device_id=(seq, peer),
            device_id_type=MESH,
        )
        copy.start()
        copies.append(copy)
    for copy in copies:
        copy.wait()
    out_ref[...] = held[...]


def hand_over(x, groups):
    count = x.shape[0]
    shape = (groups, *x.shape)
    return pl.pallas_call(
        lambda *refs: hand_over_kernel(count, groups, *refs),
        in_specs=[pl.BlockSpec(memory_space=pltpu.VMEM)],
        out_specs=pl.BlockSpec(memory_space=pltpu.VMEM),
        out_shape=jax.ShapeDtypeStruct(shape, jnp.bfloat16),
        scratch_shapes=[
            pltpu.VMEM(shape, jnp.bfloat16),
            pltpu.SemaphoreType.DMA((count,)),
            pltpu.SemaphoreType.DMA((count,)),
            pltpu.SemaphoreType.DMA((groups - 1,)),
            pltpu.SemaphoreType.DMA((groups - 1,)),
        ],
        compiler_params=pltpu.CompilerParams(collective_id=1, has_side_effects=True),
        name="hand_over",
    )(x)


def body(
    vis_tokens,
    vis_counts,
    vis_spatial,
    enc_gain,
    enc_bias,
    enc_qkv,
    enc_proj,
    final_gain,
    final_bias,
    to_decoder,
    mask_token,
    dec_gain,
    dec_bias,
    dec_qkv,
):
    seq_count = lax.axis_size("seq")
    seq_index = lax.axis_index("seq")
    quarter = lax.axis_index("head")
    clip_index = seq_index % CLIPS
    member = seq_index // CLIPS
    slot_ids = jnp.arange(SLOTS, dtype=jnp.int32)
    starts = jnp.cumsum(vis_counts, axis=1) - vis_counts
    group_counts = lax.dynamic_index_in_dim(vis_counts, clip_index, 0, keepdims=False)
    before = lax.dynamic_slice(starts, (clip_index, member), (1, 1))[0, 0]

    enc_q, enc_kv = encoder_projections(vis_tokens, enc_gain, enc_bias, jnp.swapaxes(enc_qkv, 1, 2))
    before_ids = (member - jnp.arange(GROUP, dtype=jnp.int32)) % GROUP
    near = before_ids[:, None] == jnp.arange(GROUP, dtype=jnp.int32)[None, :]
    near_counts = jnp.sum(jnp.where(near, group_counts[None, :], 0), axis=1)
    live = (slot_ids[None, :] < near_counts[:, None]).reshape(1, GROUP * SLOTS)

    frame_ids = jnp.arange(S, dtype=jnp.int32)
    flags = jnp.any(vis_spatial[:, :, None] == frame_ids[None, None, :], axis=1)
    kept = jnp.where(flags, 0.0, 1.0)
    keep_rows = kept.reshape(CLIPS, CHUNKS, CHUNK).transpose(1, 0, 2)
    lane_clip = jnp.arange(CLIPS * HEAD, dtype=jnp.int32) // HEAD
    clip_lanes = (lane_clip[None, :] == jnp.arange(CLIPS)[:, None]).astype(jnp.float32)
    keep = jnp.dot(kept.T, clip_lanes, precision=lax.Precision.HIGHEST).reshape(CHUNKS, CHUNK, CLIPS * HEAD)
    offset_rows = (1.0 - keep_rows) * floor_score
    offsets = jnp.repeat(offset_rows, OWNVIS, axis=1)
    wkv = jnp.concatenate([dec_qkv[1], dec_qkv[2]], axis=1)

    own_ids = jnp.arange(OWN, dtype=jnp.int32)
    own_frame, own_place = own_ids // BLOCK, own_ids % BLOCK
    scale = 1.0 / math.sqrt(HEAD)
    head_of_lane = jnp.arange(2 * HEAD, dtype=jnp.int32) // HEAD

    def split_heads(q):
        q = (q.astype(jnp.bfloat16) * jnp.bfloat16(scale))[None]
        return jnp.where(jnp.arange(2)[:, None, None] == head_of_lane[None, None, :], q, jnp.bfloat16(0))

    own_spatial = lax.dynamic_slice(vis_spatial, (0, seq_index * VB), (CLIPS, VB))
    fine = jnp.concatenate([seq_index * BLOCK + jnp.arange(BLOCK, dtype=jnp.int32), own_spatial.reshape(-1)])
    a1, a2, b1, b2 = angle_tables(jnp.arange(FRAMES, dtype=jnp.int32) * S, fine)
    own_table = a1[:, None, :] * b1[None, :BLOCK] + a2[:, None, :] * b2[None, :BLOCK]
    own_table = own_table.reshape(OWN, DD) + mask_token[None, :]
    base_in = layer_norm(own_table, dec_gain, dec_bias).astype(jnp.bfloat16)
    q_masked = split_heads(jnp.dot(base_in, dec_qkv[0], preferred_element_type=jnp.float32))
    b1, b2 = b1[BLOCK:].reshape(CLIPS, 1, VB, DD), b2[BLOCK:].reshape(CLIPS, 1, VB, DD)
    vis_table = a1[None, :, None, :] * b1 + a2[None, :, None, :] * b2
    k_masked, v_masked, *base, others = masked_part(
        mask_token, dec_gain, dec_bias, wkv, keep, q_masked[:1], keep_rows, enc_kv
    )
    source = (slot_ids - before) % SLOTS
    turn = (source[:, None] == slot_ids[None, :]).astype(jnp.bfloat16)
    turn_part = lax.dynamic_slice_in_dim(turn, quarter * QUARTER, QUARTER, 0)
    tokens_part = jnp.dot(turn_part, vis_tokens, preferred_element_type=jnp.float32)
    tokens_part, vis_table, turn = lax.optimization_barrier((tokens_part, vis_table, turn))

    parts = encoder_attention(enc_q, enc_kv, others, jnp.where(live, 0.0, floor_score), turn, enc_proj)
    encoded = finish_encoder(parts, tokens_part, final_gain, final_bias, to_decoder)

    groups = lax.axis_size("head")
    blocks = jnp.pad(encoded.reshape(seq_count, VB * DD // CHUNK, CHUNK), ((0, 0), (0, 4), (0, 0)))
    arrived = hand_over(blocks, groups)[:, :, : VB * DD // CHUNK]
    a_ids = jnp.arange(groups, dtype=jnp.int32)[:, None, None]
    from_ids = jnp.arange(seq_count, dtype=jnp.int32)
    i_ids = jnp.arange(VB, dtype=jnp.int32)[None, None, :]
    from_start = starts.T.reshape(-1)[None, :, None]
    from_count = vis_counts.T.reshape(-1)[None, :, None]
    row = a_ids * VSP + seq_index * VB + i_ids
    offset_in = (row - from_start) % SLOTS
    token = from_start + offset_in
    frame = token // VSP
    target = (from_ids % CLIPS)[None, :, None] * OWNVIS + frame * VB + i_ids
    target = jnp.where(offset_in < from_count, target, -1).reshape(-1)
    pick = (jnp.arange(CLIPS * OWNVIS, dtype=jnp.int32)[:, None] == target[None, :]).astype(jnp.bfloat16)
    own_encoded = jnp.dot(pick, arrived.reshape(-1, DD), preferred_element_type=jnp.float32)

    vis_in = vis_table.reshape(CLIPS * OWNVIS, DD) + own_encoded
    vis_in = layer_norm(vis_in, dec_gain, dec_bias).astype(jnp.bfloat16)
    vis_q, vis_k, vis_v = [jnp.dot(vis_in, dec_qkv[i], preferred_element_type=jnp.float32) for i in range(3)]
    vis_kv = jnp.concatenate([vis_k, vis_v], axis=1).astype(jnp.bfloat16).reshape(CLIPS, OWNVIS, 4 * HEAD)
    all_kv = lax.all_gather(vis_kv, "seq")
    q_visible = split_heads(vis_q)

    def by_clip(_):
        offset = jnp.broadcast_to(
            offset_rows.transpose(1, 0, 2)[:, :, None, :], (CLIPS, CHUNKS, SLOW_ROWS, CHUNK)
        )
        accs, ms, ls = lax.map(lambda x: single_attention(q_masked, k_masked, v_masked, x, SLOW_ROWS), offset)
        acc = accs[0]
        for clip in range(1, CLIPS):
            acc = jnp.where(lane_clip[None, None, :] == clip, accs[clip], acc)
        return acc, jnp.swapaxes(ms, 0, 1), jnp.swapaxes(ls, 0, 1)

    later, _ = lax.optimization_barrier((q_masked[1:], vis_kv))
    second = base_attention(1, later, k_masked, v_masked, keep_rows)
    base = [jnp.concatenate([x, y]) for x, y in zip(base, second)]

    def shared(_):
        return base[0], jnp.broadcast_to(base[1][:, None], (2, CLIPS, OWN, CHUNK)), base[2]

    vanishing = jnp.min(jnp.sum(base[2], axis=-1)) < 2.0**-60
    base = lax.cond(vanishing, by_clip, shared, None)

    single = single_attention(q_visible, k_masked, v_masked, offsets, CLIPS * OWNVIS)

    token_ids = jnp.arange(OWNVIS, dtype=jnp.int32)
    token_place = jnp.repeat(own_spatial[:, None, :] - seq_index * BLOCK, FRAMES, axis=1).reshape(CLIPS, 1, OWNVIS)
    place = (own_frame[None, :, None] == (token_ids // VB)[None, None, :]) & (own_place[None, :, None] == token_place)
    place = place.astype(jnp.float32)

    out = join_attention(q_masked, q_visible, all_kv, base, single, place)
    return out.reshape(CLIPS, FRAMES, BLOCK, 2 * HEAD)


def solution(mesh):
    in_specs = (
        P("seq", None),
        P(),
        P(),
        P(),
        P(),
        P(None, None, "head"),
        P("head", None),
        P(),
        P(),
        P(),
        P(),
        P(),
        P(),
        P(None, None, "head"),
    )
    out_specs = P(None, None, "seq", "head")
    return jax.shard_map(body, mesh=mesh, in_specs=in_specs, out_specs=out_specs, check_vma=False)
```

```python
import math

import jax
import jax.numpy as jnp
from jax import lax
from jax.experimental import pallas as pl
from jax.experimental.pallas import tpu as pltpu
from jax.sharding import PartitionSpec as P

D = 1408
HEADS = 16
DD = 512
DHEADS = 8
S = 1024
BLOCK = 32
VB = 3
GROUP = 8
L = 16384
VSP = 96
VIS = 1536
FRAMES = L // S
CLIPS = 4
SLOTS = 384
QUARTER = 96
CHUNK = 128
CHUNKS = S // CHUNK
KEYS = CHUNK * FRAMES
OWN = FRAMES * BLOCK
OWNVIS = FRAMES * VB
HEAD = DD // DHEADS
LOG2E = 1.4426950408889634
epsilon = 1e-06
floor_score = -1e30
NT = (((1,), (1,)), ((), ()))


def layer_norm(values, gain_row, bias_row):
    centre = jnp.mean(values, axis=-1, keepdims=True)
    centred = values - centre
    spread = jnp.mean(centred * centred, axis=-1, keepdims=True)
    return centred * lax.rsqrt(spread + epsilon) * gain_row + bias_row


def frequencies():
    column_ids = jnp.arange(DD, dtype=jnp.int32)
    exponent = (2 * (column_ids // 2)).astype(jnp.float32) / DD
    return column_ids % 2 == 0, jnp.exp(exponent * -math.log(10000.0))


def sinusoid(positions):
    even, frequency = frequencies()
    angles = positions.astype(jnp.float32)[:, None] * frequency[None, :]
    return jnp.where(even[None, :], jnp.sin(angles), jnp.cos(angles))


TILES = 8


def table_kernel(a1, a2, b1, b2, token, gain, bias, wkv, keep, k_ref, v_ref):
    lanes = lax.broadcasted_iota(jnp.int32, (1, 2 * HEAD), 1)

    def some(part, carry):
        for unrolled in range(TILES // 2):
            tile = part * (TILES // 2) + unrolled
            rows, one = pl.ds(pl.multiple_of(tile * CHUNK, CHUNK), CHUNK), pl.ds(tile, 1)
            x = a1[0, one, :] * b1[...] + a2[0, one, :] * b2[...] + token[...]
            h = layer_norm(x, gain[...], bias[...]).astype(jnp.bfloat16)
            kv = jnp.dot(h, wkv[...], preferred_element_type=jnp.float32)
            k_ref[rows, :] = kv[:, : 2 * HEAD].astype(jnp.bfloat16)
            v = kv[:, 2 * HEAD :]
            turned = pltpu.roll(v, HEAD, 1)
            for head in range(2):
                twice = jnp.where((lanes < HEAD) == (head == 0), v, turned)
                v_ref[head, rows, :] = (jnp.concatenate([twice, twice], axis=1) * keep[0]).astype(jnp.bfloat16)
        return carry

    lax.fori_loop(0, 2, some, 0)


def angle_tables(coarse, fine):
    even, frequency = frequencies()
    angle_a = coarse.astype(jnp.float32)[:, None] * frequency[None, :]
    angle_b = fine.astype(jnp.float32)[:, None] * frequency[None, :]
    sin_a, cos_a = jnp.sin(angle_a), jnp.cos(angle_a)
    a1 = jnp.where(even[None, :], sin_a, cos_a)
    a2 = jnp.where(even[None, :], cos_a, -sin_a)
    return lax.optimization_barrier((a1, a2, jnp.cos(angle_b), jnp.sin(angle_b)))


def make_tables(mask_token, dec_gain, dec_bias, wkv, keep):
    coarse = (jnp.arange(FRAMES) * S)[None, :] + (jnp.arange(CHUNKS) * CHUNK)[:, None]
    a1, a2, b1, b2 = angle_tables(coarse.reshape(-1), jnp.arange(CHUNK))
    a1, a2 = a1.reshape(-1, TILES, DD), a2.reshape(-1, TILES, DD)
    steps = a1.shape[0]
    per_chunk = steps // CHUNKS
    whole = lambda *shape: pl.BlockSpec(shape, lambda i: (0,) * len(shape))
    return pl.pallas_call(
        table_kernel,
        grid=(steps,),
        in_specs=[
            pl.BlockSpec((1, TILES, DD), lambda i: (i, 0, 0)),
            pl.BlockSpec((1, TILES, DD), lambda i: (i, 0, 0)),
            whole(CHUNK, DD),
            whole(CHUNK, DD),
            whole(1, DD),
            whole(1, DD),
            whole(1, DD),
            whole(DD, 4 * HEAD),
            pl.BlockSpec((1, CHUNK, CLIPS * HEAD), lambda i: (i // per_chunk, 0, 0)),
        ],
        out_specs=[
            pl.BlockSpec((TILES * CHUNK, 2 * HEAD), lambda i: (i, 0)),
            pl.BlockSpec((2, TILES * CHUNK, CLIPS * HEAD), lambda i: (0, i, 0)),
        ],
        out_shape=[
            jax.ShapeDtypeStruct((L, 2 * HEAD), jnp.bfloat16),
            jax.ShapeDtypeStruct((2, L, CLIPS * HEAD), jnp.bfloat16),
        ],
        cost_estimate=pl.CostEstimate(flops=20 * 10**9, bytes_accessed=25 * 10**6, transcendentals=0),
        name="masked_tables",
    )(a1, a2, b1, b2, mask_token[None], dec_gain[None], dec_bias[None], wkv, keep)


def lane_tiles(x):
    total = x[:, :CHUNK]
    for tile in range(1, x.shape[1] // CHUNK):
        total = total + x[:, tile * CHUNK : (tile + 1) * CHUNK]
    return total


BASE_ROWS = 128
JOIN_ROWS = 512
SLOW_ROWS = 16


def base_kernel(q_ref, k_ref, v_ref, keep_ref, acc_ref, m_ref, l_ref):
    first = pl.program_id(1) == 0

    @pl.when(first)
    def _():
        acc_ref[...] = jnp.zeros_like(acc_ref)
        l_ref[...] = jnp.zeros_like(l_ref)
        m_ref[...] = jnp.full_like(m_ref, floor_score)

    for start in range(0, OWN, BASE_ROWS):
        rows = pl.ds(start, BASE_ROWS)
        s = lax.dot_general(q_ref[0, rows, :], k_ref[...], NT, preferred_element_type=jnp.float32)
        old = m_ref[0, rows, :]
        new = jnp.maximum(old, jnp.max(s, axis=1, keepdims=True))
        factor = jnp.exp2((old - new) * LOG2E)
        e = jnp.exp2((s - new[:, :1]) * LOG2E)
        total = lane_tiles(e)
        for clip in range(CLIPS):
            l_ref[0, clip, rows, :] = l_ref[0, clip, rows, :] * factor + total * keep_ref[0, clip : clip + 1, :]
        m_ref[0, rows, :] = new
        update = jnp.dot(e.astype(jnp.bfloat16), v_ref[0], preferred_element_type=jnp.float32)
        acc_ref[0, rows, :] = acc_ref[0, rows, :] * jnp.concatenate([factor, factor], axis=1) + update


def base_attention(q, k, v4, keep_rows):
    return pl.pallas_call(
        base_kernel,
        grid=(2, CHUNKS),
        in_specs=[
            pl.BlockSpec((1, OWN, 2 * HEAD), lambda h, j: (h, 0, 0)),
            pl.BlockSpec((KEYS, 2 * HEAD), lambda h, j: (j, 0)),
            pl.BlockSpec((1, KEYS, CLIPS * HEAD), lambda h, j: (h, j, 0)),
            pl.BlockSpec((1, CLIPS, CHUNK), lambda h, j: (j, 0, 0)),
        ],
        out_specs=[
            pl.BlockSpec((1, OWN, CLIPS * HEAD), lambda h, j: (h, 0, 0)),
            pl.BlockSpec((1, OWN, CHUNK), lambda h, j: (h, 0, 0)),
            pl.BlockSpec((1, CLIPS, OWN, CHUNK), lambda h, j: (h, 0, 0, 0)),
        ],
        out_shape=[
            jax.ShapeDtypeStruct((2, OWN, CLIPS * HEAD), jnp.float32),
            jax.ShapeDtypeStruct((2, OWN, CHUNK), jnp.float32),
            jax.ShapeDtypeStruct((2, CLIPS, OWN, CHUNK), jnp.float32),
        ],
        cost_estimate=pl.CostEstimate(flops=25 * 10**9, bytes_accessed=25 * 10**6, transcendentals=17 * 10**6),
        name="masked_queries",
    )(q, k, v4, keep_rows)


def single_kernel(q_ref, k_ref, v_ref, offset_ref, acc_ref, m_ref, l_ref):
    @pl.when(pl.program_id(1) == 0)
    def _():
        acc_ref[...] = jnp.zeros_like(acc_ref)
        l_ref[...] = jnp.zeros_like(l_ref)
        m_ref[...] = jnp.full_like(m_ref, floor_score)

    single_chunk(q_ref, k_ref, v_ref, offset_ref, acc_ref, m_ref, l_ref)


def single_chunk(q_ref, k_ref, v_ref, offset_ref, acc_ref, m_ref, l_ref):
    offset = jnp.concatenate([offset_ref[0]] * FRAMES, axis=1)
    for head in range(2):
        s = lax.dot_general(q_ref[head], k_ref[...], NT, preferred_element_type=jnp.float32) + offset
        old = m_ref[head]
        new = jnp.maximum(old, jnp.max(s, axis=1, keepdims=True))
        factor = jnp.exp2((old - new) * LOG2E)
        e = jnp.exp2((s - new[:, :1]) * LOG2E)
        l_ref[head] = l_ref[head] * factor + lane_tiles(e)
        m_ref[head] = new
        update = jnp.dot(e.astype(jnp.bfloat16), v_ref[head], preferred_element_type=jnp.float32)
        acc_ref[head] = acc_ref[head] * jnp.concatenate([factor, factor], axis=1) + update


def single_attention(q, k, v4, offsets, block):
    rows = q.shape[1]
    blocks = rows // block
    offset_map = (lambda r, j: (j, r, 0)) if offsets.shape[1] == rows else (lambda r, j: (j, 0, 0))
    out_spec = lambda width: pl.BlockSpec((2, block, width), lambda r, j: (0, r, 0))
    return pl.pallas_call(
        single_kernel,
        grid=(blocks, CHUNKS),
        in_specs=[
            pl.BlockSpec((2, block, 2 * HEAD), lambda r, j: (0, r, 0)),
            pl.BlockSpec((KEYS, 2 * HEAD), lambda r, j: (j, 0)),
            pl.BlockSpec((2, KEYS, CLIPS * HEAD), lambda r, j: (0, j, 0)),
            pl.BlockSpec((1, block, CHUNK), offset_map),
        ],
        out_specs=[out_spec(CLIPS * HEAD), out_spec(CHUNK), out_spec(CHUNK)],
        out_shape=[
            jax.ShapeDtypeStruct((2, rows, CLIPS * HEAD), jnp.float32),
            jax.ShapeDtypeStruct((2, rows, CHUNK), jnp.float32),
            jax.ShapeDtypeStruct((2, rows, CHUNK), jnp.float32),
        ],
        cost_estimate=pl.CostEstimate(flops=20 * 10**9, bytes_accessed=25 * 10**6, transcendentals=6 * 10**6),
        name="masked_queries_by_clip",
    )(q, k, v4, offsets)


SIDE = 4
MESH = pl.DeviceIdType.MESH


def spread_kernel(
    q_ref, k_ref, v_ref, offset_ref, own_k, own_v, acc_ref, m_ref, l_ref, all_k, all_v, local, send_1, recv_1, send_2,
    recv_2, send_3, recv_3,
):
    step = pl.program_id(1)
    seq, head = lax.axis_index("seq"), lax.axis_index("head")
    core = lax.rem(seq, 2)
    x, y = seq // (2 * SIDE), lax.rem(seq // 2, SIDE)
    arrays = ((0, own_k, all_k), (1, own_v, all_v))

    def chip(kind, along, across):
        a, b = (along, across) if kind == 0 else (across, along)
        return lax.rem(x + a + SIDE, SIDE) * SIDE + lax.rem(y + b + SIDE, SIDE)

    def remote(source, target, place, sends, recvs, index, peer_chip, peer_core):
        return pltpu.make_async_remote_copy(
            src_ref=source,
            dst_ref=target.at[place, core],
            send_sem=sends.at[index],
            recv_sem=recvs.at[index],
            device_id=(peer_chip * 2 + peer_core, head),
            device_id_type=MESH,
        )

    def first(kind, own, whole, d):
        return remote(own, whole, chip(kind, 0, 0), send_1, recv_1, kind * 3 + d - 1, chip(kind, d, 0), core)

    def second(kind, own, whole, e, d):
        place = chip(kind, -d, 0)
        source = own if d == 0 else whole.at[place, core]
        index = kind * 12 + (e - 1) * SIDE + d
        return remote(source, whole, place, send_2, recv_2, index, chip(kind, 0, e), core)

    def third(kind, own, whole, e, d):
        place = chip(kind, -d, -e)
        source = own if d == 0 and e == 0 else whole.at[place, core]
        index = kind * 16 + e * SIDE + d
        return remote(source, whole, place, send_3, recv_3, index, chip(kind, 0, 0), 1 - core)

    def keep(kind, own, whole):
        return pltpu.make_async_copy(own, whole.at[chip(kind, 0, 0), core], local.at[kind])

    @pl.when(step == 0)
    def _():
        barrier = pltpu.get_barrier_semaphore()
        for d in range(1, SIDE):
            for kind in range(2):
                peer = (chip(kind, d, 0) * 2 + core, head)
                pl.semaphore_signal(barrier, inc=1, device_id=peer, device_id_type=MESH)
        peer = (chip(0, 0, 0) * 2 + 1 - core, head)
        pl.semaphore_signal(barrier, inc=1, device_id=peer, device_id_type=MESH)
        pl.semaphore_wait(barrier, 7)
        for kind, own, whole in arrays:
            for d in range(1, SIDE):
                first(kind, own, whole, d).start()
            third(kind, own, whole, 0, 0).start()
            keep(kind, own, whole).start()
        acc_ref[...] = jnp.zeros_like(acc_ref)
        l_ref[...] = jnp.zeros_like(l_ref)
        m_ref[...] = jnp.full_like(m_ref, floor_score)

    @pl.when(step == 3)
    def _():
        for kind, own, whole in arrays:
            for d in range(1, SIDE):
                first(kind, own, whole, d).wait()
            for d in range(SIDE):
                for e in range(1, SIDE):
                    second(kind, own, whole, e, d).start()
            for d in range(1, SIDE):
                third(kind, own, whole, 0, d).start()

    single_chunk(q_ref, k_ref, v_ref, offset_ref, acc_ref, m_ref, l_ref)

    @pl.when(step == CHUNKS - 1)
    def _():
        for e in range(1, SIDE):
            for d in range(SIDE):
                for kind, own, whole in arrays:
                    second(kind, own, whole, e, d).wait()
                    third(kind, own, whole, e, d).start()
        for kind, own, whole in arrays:
            keep(kind, own, whole).wait()
            for e in range(SIDE):
                for d in range(SIDE):
                    third(kind, own, whole, e, d).wait()


def spread_attention(q, k, v4, offsets, own_k, own_v):
    rows = q.shape[1]
    out_spec = lambda width: pl.BlockSpec((2, rows, width), lambda r, j: (0, 0, 0))
    everyone = jax.ShapeDtypeStruct((SIDE * SIDE, 2, *own_k.shape), jnp.bfloat16)
    sems = lambda n: pltpu.SemaphoreType.DMA((n,))
    *sums, all_k, all_v = pl.pallas_call(
        spread_kernel,
        grid=(1, CHUNKS),
        in_specs=[
            pl.BlockSpec((2, rows, 2 * HEAD), lambda r, j: (0, 0, 0)),
            pl.BlockSpec((KEYS, 2 * HEAD), lambda r, j: (j, 0)),
            pl.BlockSpec((2, KEYS, CLIPS * HEAD), lambda r, j: (0, j, 0)),
            pl.BlockSpec((1, rows, CHUNK), lambda r, j: (j, 0, 0)),
            pl.BlockSpec(memory_space=pltpu.VMEM),
            pl.BlockSpec(memory_space=pltpu.VMEM),
        ],
        out_specs=[
            out_spec(CLIPS * HEAD),
            out_spec(CHUNK),
            out_spec(CHUNK),
            pl.BlockSpec(memory_space=pl.ANY),
            pl.BlockSpec(memory_space=pl.ANY),
        ],
        out_shape=[
            jax.ShapeDtypeStruct((2, rows, CLIPS * HEAD), jnp.float32),
            jax.ShapeDtypeStruct((2, rows, CHUNK), jnp.float32),
            jax.ShapeDtypeStruct((2, rows, CHUNK), jnp.float32),
            everyone,
            everyone,
        ],
        scratch_shapes=[sems(2), sems(6), sems(6), sems(24), sems(24), sems(32), sems(32)],
        compiler_params=pltpu.CompilerParams(collective_id=2, has_side_effects=True),
        cost_estimate=pl.CostEstimate(flops=20 * 10**9, bytes_accessed=25 * 10**6, transcendentals=6 * 10**6),
        name="visible_queries",
    )(q, k, v4, offsets, own_k, own_v)
    shape = (2 * SIDE * SIDE, CLIPS, OWNVIS, 2 * HEAD)
    return sums, all_k.reshape(shape), all_v.reshape(shape)


def own_columns(acc, clip, head):
    piece = jnp.where(clip >= 2, acc[:, CHUNK:], acc[:, :CHUNK])
    return jnp.where(clip % 2 == head, piece, pltpu.roll(piece, HEAD, 1))


def join(q, k, v, acc, m, l):
    s = lax.dot_general(q, k, NT, preferred_element_type=jnp.float32)
    new = jnp.maximum(m, jnp.max(s, axis=1, keepdims=True))
    e = jnp.exp2((s - new[:, :1]) * LOG2E)
    factor = jnp.exp2((m - new) * LOG2E)
    total = jnp.sum(l * factor + lane_tiles(e), axis=1, keepdims=True)
    update = jnp.dot(e.astype(jnp.bfloat16), v, preferred_element_type=jnp.float32)
    return (acc * factor + update) / total


def join_kernel(qb_ref, qv_ref, k_ref, v_ref, accb_ref, mb_ref, lb_ref, accv_ref, mv_ref, lv_ref, place_ref, out_ref):
    clip = pl.program_id(0)
    lanes = lax.broadcasted_iota(jnp.int32, (1, 2 * HEAD), 1)
    k = k_ref[:, 0].reshape(VIS, 2 * HEAD)
    v = v_ref[:, 0].reshape(VIS, 2 * HEAD)
    place = place_ref[0]
    seen = jnp.sum(place, axis=1, keepdims=True) > 0.5
    for head in range(2):
        mine = (lanes // HEAD) == head
        vis = join(
            qv_ref[head, 0], k, v, own_columns(accv_ref[head, 0], clip, head), mv_ref[head, 0], lv_ref[head, 0]
        ).astype(jnp.bfloat16)
        for start in range(0, OWN, JOIN_ROWS):
            rows = pl.ds(start, JOIN_ROWS)
            base = join(
                qb_ref[head, rows, :],
                k,
                v,
                own_columns(accb_ref[head, rows, :], clip, head),
                mb_ref[head, 0, rows, :],
                lb_ref[head, 0, rows, :],
            )
            spread = jnp.dot(
                place[start : start + JOIN_ROWS].astype(jnp.bfloat16), vis, preferred_element_type=jnp.float32
            )
            value = jnp.where(seen[start : start + JOIN_ROWS], spread, base).astype(jnp.bfloat16)
            if head == 0:
                out_ref[0, rows, :] = value
            else:
                out_ref[0, rows, :] = jnp.where(mine, value, out_ref[0, rows, :])


def join_attention(qb, qv, k, v, base, single, place):
    seq_count = k.shape[0]
    accb, mb, lb = base
    accv, mv, lv = [x.reshape(2, CLIPS, OWNVIS, -1) for x in single]
    vis_spec = lambda width: pl.BlockSpec((2, 1, OWNVIS, width), lambda c: (0, c, 0, 0))
    return pl.pallas_call(
        join_kernel,
        grid=(CLIPS,),
        in_specs=[
            pl.BlockSpec((2, OWN, 2 * HEAD), lambda c: (0, 0, 0)),
            vis_spec(2 * HEAD),
            pl.BlockSpec((seq_count, 1, OWNVIS, 2 * HEAD), lambda c: (0, c, 0, 0)),
            pl.BlockSpec((seq_count, 1, OWNVIS, 2 * HEAD), lambda c: (0, c, 0, 0)),
            pl.BlockSpec((2, OWN, CLIPS * HEAD), lambda c: (0, 0, 0)),
            pl.BlockSpec((2, 1, OWN, CHUNK), lambda c: (0, c, 0, 0)),
            pl.BlockSpec((2, 1, OWN, CHUNK), lambda c: (0, c, 0, 0)),
            vis_spec(CLIPS * HEAD),
            vis_spec(CHUNK),
            vis_spec(CHUNK),
            pl.BlockSpec((1, OWN, OWNVIS), lambda c: (c, 0, 0)),
        ],
        out_specs=pl.BlockSpec((1, OWN, 2 * HEAD), lambda c: (c, 0, 0)),
        out_shape=jax.ShapeDtypeStruct((CLIPS, OWN, 2 * HEAD), jnp.bfloat16),
        cost_estimate=pl.CostEstimate(flops=8 * 10**9, bytes_accessed=10**7, transcendentals=7 * 10**6),
        name="join_visible_keys",
    )(qb, qv.reshape(2, CLIPS, OWNVIS, -1), k, v, accb, mb, lb, accv, mv, lv, place)


def project_kernel(x_ref, gain_ref, bias_ref, w_ref, q_ref, kv_ref, h_ref):
    part = pl.program_id(0)

    @pl.when(part == 0)
    def _():
        gain, bias = gain_ref[...].reshape(1, D), bias_ref[...].reshape(1, D)
        h_ref[...] = layer_norm(x_ref[...].astype(jnp.float32), gain, bias).astype(jnp.bfloat16)

    @pl.when(part == 2)
    def _():
        q_ref[...] = lax.dot_general(h_ref[...], w_ref[0], NT, preferred_element_type=jnp.float32).astype(jnp.bfloat16)

    @pl.when(part < 2)
    def _():
        kv_ref[0] = lax.dot_general(w_ref[0], h_ref[...], NT, preferred_element_type=jnp.float32).astype(jnp.bfloat16)


def encoder_projections(x, gain, bias, w):
    slots, width = x.shape[0], w.shape[1]
    return pl.pallas_call(
        project_kernel,
        grid=(3,),
        in_specs=[
            pl.BlockSpec((slots, D), lambda i: (0, 0)),
            pl.BlockSpec((D,), lambda i: (0,)),
            pl.BlockSpec((D,), lambda i: (0,)),
            pl.BlockSpec((1, width, D), lambda i: ((i + 1) % 3, 0, 0)),
        ],
        out_specs=[
            pl.BlockSpec((slots, width), lambda i: (0, 0)),
            pl.BlockSpec((1, width, slots), lambda i: (jnp.minimum(i, 1), 0, 0)),
        ],
        out_shape=[
            jax.ShapeDtypeStruct((slots, width), jnp.bfloat16),
            jax.ShapeDtypeStruct((2, width, slots), jnp.bfloat16),
        ],
        scratch_shapes=[pltpu.VMEM((slots, D), jnp.bfloat16)],
        cost_estimate=pl.CostEstimate(flops=12 * 10**8, bytes_accessed=5 * 10**6, transcendentals=0),
        name="encoder_projections",
    )(x, gain, bias, w)


def encoder_kernel(q_ref, kv_ref, offset_ref, turn_ref, proj_ref, out_ref, context_ref):
    width = q_ref.shape[1]
    head_size = D // HEADS
    scale = LOG2E / math.sqrt(head_size)
    sums = []
    for low, high, heads in ((0, 256, (0, 1)), (128, width, (2, 3))):
        lanes = lax.broadcasted_iota(jnp.int32, (1, high - low), 1) + low
        window = q_ref[:, low:high]
        result = None
        for head in heads:
            mine = (lanes >= head * head_size) & (lanes < (head + 1) * head_size)
            q = jnp.where(mine, window, jnp.zeros_like(window))
            s = [jnp.dot(q, kv_ref[g, 0, low:high, :], preferred_element_type=jnp.float32) for g in range(GROUP)]
            s = jnp.concatenate(s, axis=1) * scale + offset_ref[...]
            e = jnp.exp2(s - jnp.max(s, axis=1, keepdims=True))
            total = jnp.sum(lane_tiles(e), axis=1, keepdims=True)
            e = e.astype(jnp.bfloat16)
            context = None
            for g in range(GROUP):
                piece = lax.dot_general(
                    e[:, g * SLOTS : (g + 1) * SLOTS],
                    kv_ref[g, 1, low:high, :],
                    NT,
                    preferred_element_type=jnp.float32,
                )
                context = piece if context is None else context + piece
            context = jnp.where(mine, context / total, 0.0)
            result = context if result is None else result + context
        sums.append(result)
    context_ref[:, :128] = sums[0][:, :128].astype(jnp.bfloat16)
    context_ref[:, 128:256] = (sums[0][:, 128:] + sums[1][:, :128]).astype(jnp.bfloat16)
    context_ref[:, 256:] = sums[1][:, 128:].astype(jnp.bfloat16)
    turned = jnp.dot(turn_ref[...], context_ref[...], preferred_element_type=jnp.float32)
    turned = turned.astype(jnp.bfloat16)
    out_ref[...] = jnp.dot(turned, proj_ref[...], preferred_element_type=jnp.float32).astype(jnp.bfloat16)


def encoder_attention(q, kv, offset, turn, proj):
    return pl.pallas_call(
        encoder_kernel,
        in_specs=[pl.BlockSpec(memory_space=pltpu.VMEM)] * 5,
        out_specs=pl.BlockSpec(memory_space=pltpu.VMEM),
        out_shape=jax.ShapeDtypeStruct((q.shape[0], D), jnp.bfloat16),
        scratch_shapes=[pltpu.VMEM(q.shape, jnp.bfloat16)],
        cost_estimate=pl.CostEstimate(flops=9 * 10**9, bytes_accessed=5 * 10**6, transcendentals=5 * 10**6),
        name="encoder_attention",
    )(q, kv, offset, turn, proj)


MESH = pl.DeviceIdType.MESH


def finish_kernel(groups, parts_ref, tokens_ref, gain_ref, bias_ref, dec_ref, out_ref, got, send, recv):
    seq, head = lax.axis_index("seq"), lax.axis_index("head")
    barrier = pltpu.get_barrier_semaphore()
    for step in range(1, groups):
        peer = lax.rem(head + step, groups)
        pl.semaphore_signal(barrier, inc=1, device_id=(seq, peer), device_id_type=MESH)
    pl.semaphore_wait(barrier, groups - 1)
    copies = []
    for step in range(1, groups):
        peer = lax.rem(head + step, groups)
        copy = pltpu.make_async_remote_copy(
            src_ref=parts_ref.at[peer],
            dst_ref=got.at[step - 1],
            send_sem=send.at[step - 1],
            recv_sem=recv.at[step - 1],
            device_id=(seq, peer),
            device_id_type=MESH,
        )
        copy.start()
        copies.append(copy)
    total = tokens_ref[...] + parts_ref[head].astype(jnp.float32)
    for step in range(1, groups):
        copies[step - 1].wait()
        total = total + got[step - 1].astype(jnp.float32)
    gain, bias = gain_ref[...].reshape(1, D), bias_ref[...].reshape(1, D)
    rows = layer_norm(total, gain, bias).astype(jnp.bfloat16)
    out_ref[...] = jnp.dot(rows, dec_ref[...], preferred_element_type=jnp.float32).astype(jnp.bfloat16)


def finish_encoder(parts, tokens, gain, bias, to_decoder):
    groups = parts.shape[0] // QUARTER
    return pl.pallas_call(
        lambda *refs: finish_kernel(groups, *refs),
        in_specs=[pl.BlockSpec(memory_space=pltpu.VMEM)] * 5,
        out_specs=pl.BlockSpec(memory_space=pltpu.VMEM),
        out_shape=jax.ShapeDtypeStruct((QUARTER, DD), jnp.bfloat16),
        scratch_shapes=[
            pltpu.VMEM((groups - 1, QUARTER, D), jnp.bfloat16),
            pltpu.SemaphoreType.DMA((groups - 1,)),
            pltpu.SemaphoreType.DMA((groups - 1,)),
        ],
        compiler_params=pltpu.CompilerParams(collective_id=0, has_side_effects=True),
        cost_estimate=pl.CostEstimate(flops=2 * 10**8, bytes_accessed=3 * 10**6, transcendentals=0),
        name="finish_encoder",
    )(parts.reshape(groups, QUARTER, D), tokens, gain, bias, to_decoder)


def hand_over_kernel(count, groups, x_ref, out_ref, held, send, recv, spread_send, spread_recv):
    seq, head = lax.axis_index("seq"), lax.axis_index("head")
    barrier = pltpu.get_barrier_semaphore()

    def greet(step, carry):
        peer = lax.rem(seq + step, count)
        pl.semaphore_signal(barrier, inc=1, device_id=(peer, head), device_id_type=MESH)
        return carry

    lax.fori_loop(1, count, greet, 0)
    for step in range(1, groups):
        peer = lax.rem(head + step, groups)
        pl.semaphore_signal(barrier, inc=1, device_id=(seq, peer), device_id_type=MESH)
    pl.semaphore_wait(barrier, count + groups - 2)

    def copy_to(step):
        peer = lax.rem(seq + step, count)
        return pltpu.make_async_remote_copy(
            src_ref=x_ref.at[peer],
            dst_ref=held.at[head, seq],
            send_sem=send.at[step],
            recv_sem=recv.at[step],
            device_id=(peer, head),
            device_id_type=MESH,
        )

    def start(step, carry):
        copy_to(step).start()
        return carry

    def finish(step, carry):
        copy_to(step).wait()
        return carry

    lax.fori_loop(1, count, start, 0)
    own = pltpu.make_async_copy(x_ref.at[seq], held.at[head, seq], send.at[0])
    own.start()
    own.wait()
    lax.fori_loop(1, count, finish, 0)
    copies = []
    for step in range(1, groups):
        peer = lax.rem(head + step, groups)
        copy = pltpu.make_async_remote_copy(
            src_ref=held.at[head],
            dst_ref=held.at[head],
            send_sem=spread_send.at[step - 1],
            recv_sem=spread_recv.at[step - 1],
            device_id=(seq, peer),
            device_id_type=MESH,
        )
        copy.start()
        copies.append(copy)
    for copy in copies:
        copy.wait()
    out_ref[...] = held[...]


def hand_over(x, groups):
    count = x.shape[0]
    shape = (groups, *x.shape)
    return pl.pallas_call(
        lambda *refs: hand_over_kernel(count, groups, *refs),
        in_specs=[pl.BlockSpec(memory_space=pltpu.VMEM)],
        out_specs=pl.BlockSpec(memory_space=pltpu.VMEM),
        out_shape=jax.ShapeDtypeStruct(shape, jnp.bfloat16),
        scratch_shapes=[
            pltpu.VMEM(shape, jnp.bfloat16),
            pltpu.SemaphoreType.DMA((count,)),
            pltpu.SemaphoreType.DMA((count,)),
            pltpu.SemaphoreType.DMA((groups - 1,)),
            pltpu.SemaphoreType.DMA((groups - 1,)),
        ],
        compiler_params=pltpu.CompilerParams(collective_id=1, has_side_effects=True),
        name="hand_over",
    )(x)


def body(
    vis_tokens,
    vis_counts,
    vis_spatial,
    enc_gain,
    enc_bias,
    enc_qkv,
    enc_proj,
    final_gain,
    final_bias,
    to_decoder,
    mask_token,
    dec_gain,
    dec_bias,
    dec_qkv,
):
    seq_count = lax.axis_size("seq")
    seq_index = lax.axis_index("seq")
    quarter = lax.axis_index("head")
    clip_index = seq_index % CLIPS
    member = seq_index // CLIPS
    slot_ids = jnp.arange(SLOTS, dtype=jnp.int32)
    starts = jnp.cumsum(vis_counts, axis=1) - vis_counts
    group_counts = lax.dynamic_index_in_dim(vis_counts, clip_index, 0, keepdims=False)
    before = lax.dynamic_slice(starts, (clip_index, member), (1, 1))[0, 0]

    enc_q, enc_kv = encoder_projections(vis_tokens, enc_gain, enc_bias, jnp.swapaxes(enc_qkv, 1, 2))
    groups = [[clip + CLIPS * g for g in range(GROUP)] for clip in range(CLIPS)]
    group_kv = lax.all_gather(enc_kv, "seq", axis_index_groups=groups)
    live = (slot_ids[None, :] < group_counts[:, None]).reshape(1, GROUP * SLOTS)

    frame_ids = jnp.arange(S, dtype=jnp.int32)
    flags = jnp.any(vis_spatial[:, :, None] == frame_ids[None, None, :], axis=1)
    kept = jnp.where(flags, 0.0, 1.0)
    keep_rows = kept.reshape(CLIPS, CHUNKS, CHUNK).transpose(1, 0, 2)
    lane_clip = jnp.arange(CLIPS * HEAD, dtype=jnp.int32) // HEAD
    clip_lanes = (lane_clip[None, :] == jnp.arange(CLIPS)[:, None]).astype(jnp.float32)
    keep = jnp.dot(kept.T, clip_lanes, precision=lax.Precision.HIGHEST).reshape(CHUNKS, CHUNK, CLIPS * HEAD)
    offset_rows = (1.0 - keep_rows) * floor_score
    offsets = jnp.repeat(offset_rows, OWNVIS, axis=1)
    wkv = jnp.concatenate([dec_qkv[1], dec_qkv[2]], axis=1)
    k_masked, v_masked = make_tables(mask_token, dec_gain, dec_bias, wkv, keep)

    own_ids = jnp.arange(OWN, dtype=jnp.int32)
    own_frame, own_place = own_ids // BLOCK, own_ids % BLOCK
    scale = 1.0 / math.sqrt(HEAD)
    head_of_lane = jnp.arange(2 * HEAD, dtype=jnp.int32) // HEAD

    def split_heads(q):
        q = (q.astype(jnp.bfloat16) * jnp.bfloat16(scale))[None]
        return jnp.where(jnp.arange(2)[:, None, None] == head_of_lane[None, None, :], q, jnp.bfloat16(0))

    own_spatial = lax.dynamic_slice(vis_spatial, (0, seq_index * VB), (CLIPS, VB))
    fine = jnp.concatenate([seq_index * BLOCK + jnp.arange(BLOCK, dtype=jnp.int32), own_spatial.reshape(-1)])
    a1, a2, b1, b2 = angle_tables(jnp.arange(FRAMES, dtype=jnp.int32) * S, fine)
    own_table = a1[:, None, :] * b1[None, :BLOCK] + a2[:, None, :] * b2[None, :BLOCK]
    own_table = own_table.reshape(OWN, DD) + mask_token[None, :]
    base_in = layer_norm(own_table, dec_gain, dec_bias).astype(jnp.bfloat16)
    q_masked = split_heads(jnp.dot(base_in, dec_qkv[0], preferred_element_type=jnp.float32))
    b1, b2 = b1[BLOCK:].reshape(CLIPS, 1, VB, DD), b2[BLOCK:].reshape(CLIPS, 1, VB, DD)
    vis_table = a1[None, :, None, :] * b1 + a2[None, :, None, :] * b2
    base = base_attention(q_masked, k_masked, v_masked, keep_rows)
    source = (slot_ids - before) % SLOTS
    turn = (source[:, None] == slot_ids[None, :]).astype(jnp.bfloat16)
    turn_part = lax.dynamic_slice_in_dim(turn, quarter * QUARTER, QUARTER, 0)
    tokens_part = jnp.dot(turn_part, vis_tokens, preferred_element_type=jnp.float32)
    group_kv, base, tokens_part, vis_table, turn = lax.optimization_barrier(
        (group_kv, base, tokens_part, vis_table, turn)
    )

    def by_clip(_):
        offset = jnp.broadcast_to(
            offset_rows.transpose(1, 0, 2)[:, :, None, :], (CLIPS, CHUNKS, SLOW_ROWS, CHUNK)
        )
        accs, ms, ls = lax.map(lambda x: single_attention(q_masked, k_masked, v_masked, x, SLOW_ROWS), offset)
        acc = accs[0]
        for clip in range(1, CLIPS):
            acc = jnp.where(lane_clip[None, None, :] == clip, accs[clip], acc)
        return acc, jnp.swapaxes(ms, 0, 1), jnp.swapaxes(ls, 0, 1)

    def shared(_):
        return base[0], jnp.broadcast_to(base[1][:, None], (2, CLIPS, OWN, CHUNK)), base[2]

    vanishing = jnp.min(jnp.sum(base[2], axis=-1)) < 2.0**-60
    base = lax.cond(vanishing, by_clip, shared, None)

    parts = encoder_attention(enc_q, group_kv, jnp.where(live, 0.0, floor_score), turn, enc_proj)
    encoded = finish_encoder(parts, tokens_part, final_gain, final_bias, to_decoder)

    groups = lax.axis_size("head")
    blocks = jnp.pad(encoded.reshape(seq_count, VB * DD // CHUNK, CHUNK), ((0, 0), (0, 4), (0, 0)))
    arrived = hand_over(blocks, groups)[:, :, : VB * DD // CHUNK]
    a_ids = jnp.arange(groups, dtype=jnp.int32)[:, None, None]
    from_ids = jnp.arange(seq_count, dtype=jnp.int32)
    i_ids = jnp.arange(VB, dtype=jnp.int32)[None, None, :]
    from_start = starts.T.reshape(-1)[None, :, None]
    from_count = vis_counts.T.reshape(-1)[None, :, None]
    row = a_ids * VSP + seq_index * VB + i_ids
    offset_in = (row - from_start) % SLOTS
    token = from_start + offset_in
    frame = token // VSP
    target = (from_ids % CLIPS)[None, :, None] * OWNVIS + frame * VB + i_ids
    target = jnp.where(offset_in < from_count, target, -1).reshape(-1)
    pick = (jnp.arange(CLIPS * OWNVIS, dtype=jnp.int32)[:, None] == target[None, :]).astype(jnp.bfloat16)
    own_encoded = jnp.dot(pick, arrived.reshape(-1, DD), preferred_element_type=jnp.float32)

    vis_in = vis_table.reshape(CLIPS * OWNVIS, DD) + own_encoded
    vis_in = layer_norm(vis_in, dec_gain, dec_bias).astype(jnp.bfloat16)
    vis_q, vis_k, vis_v = [jnp.dot(vis_in, dec_qkv[i], preferred_element_type=jnp.float32) for i in range(3)]
    q_visible = split_heads(vis_q)
    single, all_k, all_v = spread_attention(
        q_visible, k_masked, v_masked, offsets, vis_k.astype(jnp.bfloat16), vis_v.astype(jnp.bfloat16)
    )

    token_ids = jnp.arange(OWNVIS, dtype=jnp.int32)
    token_place = jnp.repeat(own_spatial[:, None, :] - seq_index * BLOCK, FRAMES, axis=1).reshape(CLIPS, 1, OWNVIS)
    place = (own_frame[None, :, None] == (token_ids // VB)[None, None, :]) & (own_place[None, :, None] == token_place)
    place = place.astype(jnp.float32)

    out = join_attention(q_masked, q_visible, all_k, all_v, base, single, place)
    return out.reshape(CLIPS, FRAMES, BLOCK, 2 * HEAD)


def solution(mesh):
    in_specs = (
        P("seq", None),
        P(),
        P(),
        P(),
        P(),
        P(None, None, "head"),
        P("head", None),
        P(),
        P(),
        P(),
        P(),
        P(),
        P(),
        P(None, None, "head"),
    )
    out_specs = P(None, None, "seq", "head")
    return jax.shard_map(body, mesh=mesh, in_specs=in_specs, out_specs=out_specs, check_vma=False)
```
